256 devices in a mesh: gx: 32 (over z, x_hi, core), gy: 8 (over y, x_lo).
Axes of the slice: x: 4 (x_hi: 2, x_lo: 2; x = x_hi * 2 + x_lo), y: 4, z: 8, core: 2. Of those that a mesh axis runs over, the one named last changes fastest.
Arguments:
- features: bfloat16 [32, 8, 3, 64, 256], P('gx', 'gy'), may hold values from -6 to 6
- block_coords: int32 [32, 8, 3], P('gx', 'gy'), may hold values from 0 to 31, as said below
- block_counts: int32 [32, 8], P('gx', 'gy'), may hold values from 2 to 3, as said below
- first_weight: bfloat16 [6912, 256], replicated, may hold values from -0.078125 to 0.078125
- second_weight: bfloat16 [6912, 256], replicated, may hold values from -0.078125 to 0.078125
- cotangent: bfloat16 [32, 8, 3, 64, 256], P('gx', 'gy'), may hold values from -6 to 6
Outputs:
- output_features: float32 [32, 8, 3, 64, 256], P('gx', 'gy')
- input_grad: float32 [32, 8, 3, 64, 256], P('gx', 'gy')
- first_weight_grad: float32 [6912, 256], P('gx', 'gy')
- second_weight_grad: float32 [6912, 256], P('gx', 'gy')
The draws below stay inside these ranges and needn't reach their ends.
Inputs may be any that keep to these rules, and one draw needn't show every extreme that they name: `block_coords`: within a tile all 3 entries are distinct block positions, so slots at or past the tile's count name blocks that are not active. Slots 0 and 1 are always live and hold blocks of the lowest block layer in opposite corners of the tile's 2 x 2 block columns. `block_counts`: at least one tile holds 3 live slots in every draw.
All inputs are finite; a program needn't handle non-finite values.
Results may differ from the reference program's by a relative error of at most 0.0029.
Values may be sent and summed in bfloat16 or wider, within the bound.
A program may use at most 128 MiB of HBM per device.

```python
import math
import jax
import jax.numpy as jnp
from jax import lax

C = 256
SLAB_BLOCKS = 8
MAX_BLOCKS = 3
TILE_ROWS = 32
TILE_COLS = 8


def draw_block_counts(key, part):
    key_base, key_busy, key_pick = jax.random.split(key, 3)
    upper_bound = max(4, MAX_BLOCKS // 2 + 2)
    base_count = jax.random.randint(key_base, (TILE_ROWS, TILE_COLS), 2, upper_bound)
    busy_tiles = jax.random.randint(key_busy, (TILE_ROWS, TILE_COLS), 0, 16) == 0
    counts_drawn = jnp.where(busy_tiles, MAX_BLOCKS, jnp.minimum(base_count, MAX_BLOCKS))
    pick_tile = jax.random.randint(key_pick, (), 0, TILE_ROWS * TILE_COLS)
    flat_counts = jnp.where(jnp.arange(TILE_ROWS * TILE_COLS) == pick_tile, MAX_BLOCKS, counts_drawn.reshape(-1))
    return flat_counts.reshape(TILE_ROWS, TILE_COLS).astype(jnp.int32)


def draw_block_coords(key, part):
    positions = 4 * SLAB_BLOCKS
    tile_total = TILE_ROWS * TILE_COLS
    key_ground, key_order = jax.random.split(key)
    corner = jax.random.randint(key_ground, (tile_total,), 0, 4)
    ground_first = corner * SLAB_BLOCKS
    ground_second = (3 - corner) * SLAB_BLOCKS
    orders = jax.vmap(lambda subkey: jax.random.permutation(subkey, positions))(jax.random.split(key_order, tile_total))
    taken_mask = (orders == ground_first[:, None]) | (orders == ground_second[:, None])
    order_rank = jnp.argsort(taken_mask.astype(jnp.int32), axis=1, stable=True)
    remaining = jnp.take_along_axis(orders, order_rank, axis=1)
    chosen = jnp.concatenate([ground_first[:, None], ground_second[:, None], remaining[:, :MAX_BLOCKS - 2]], axis=1)
    return chosen.reshape(TILE_ROWS, TILE_COLS, MAX_BLOCKS).astype(jnp.int32)


def steps_of(rng, shape, cuts, least, top_value):
    def one(position, shards_of):
        steps = jax.random.uniform(jax.random.fold_in(jax.random.fold_in(rng, 6), position), (shards_of,), jnp.float32, least / len(cuts), top_value / len(cuts))
        return jnp.repeat(jnp.exp(steps), shape[position] // shards_of).reshape((-1,) + (1,) * (len(shape) - position - 1))

    loudness = one(*cuts[0])
    for cut in cuts[1:]:
        loudness = loudness * one(*cut)
    return loudness


def scatter_about(rng, dims, deviation, limit, cuts=(), kind=jnp.bfloat16):
    array = jax.random.normal(rng, dims, jnp.float32) * deviation
    if len(cuts) > 0:
        array = steps_of(rng, dims, cuts, -0.22, 0.18) * array
    return jnp.clip(array, min=-limit, max=limit).astype(kind)


def setup_inputs(seed: int = 0) -> dict:
    seeds = jax.random.split(jax.random.key(seed), 7)
    return {
        "features": scatter_about(seeds[0], (TILE_ROWS, TILE_COLS, MAX_BLOCKS, 64, C), 1.0, 6.0, ((0, 32), (1, 8))),
        "block_coords": draw_block_coords(jax.random.fold_in(seeds[6], 71), 0),
        "block_counts": draw_block_counts(jax.random.fold_in(seeds[6], 71), 0),
        "first_weight": scatter_about(seeds[3], (27 * C, C), (27 * C) ** -0.5, 0.078125),
        "second_weight": scatter_about(seeds[4], (27 * C, C), (27 * C) ** -0.5, 0.078125),
        "cotangent": scatter_about(seeds[5], (TILE_ROWS, TILE_COLS, MAX_BLOCKS, 64, C), 1.0, 6.0, ((0, 32), (1, 8))),
    }


def tile_grid(field, slot_blocks, live_count):
    positions = jnp.arange(4 * SLAB_BLOCKS, dtype=jnp.int32)
    slot_index = jnp.arange(MAX_BLOCKS, dtype=jnp.int32)
    placing = (slot_blocks[:, None] == positions[None, :]) & (slot_index < live_count)[:, None]
    blocks = jnp.einsum('sp,svc->pvc', placing.astype(jnp.float32), field.astype(jnp.float32))
    blocks = blocks.reshape(2, 2, SLAB_BLOCKS, 4, 4, 4, C).transpose(0, 3, 1, 4, 2, 5, 6)
    return blocks.reshape(8, 8, 4 * SLAB_BLOCKS, C)

def padded_tile(field, block_coords, block_counts, tile_row, tile_col):
    strips = []
    for step_row in (-1, 0, 1):
        pieces = []
        for step_col in (-1, 0, 1):
            row_near = tile_row + step_row
            col_near = tile_col + step_col
            inside = (row_near >= 0) & (row_near < TILE_ROWS) & (col_near >= 0) & (col_near < TILE_COLS)
            row_safe = jnp.clip(row_near, 0, TILE_ROWS - 1)
            col_safe = jnp.clip(col_near, 0, TILE_COLS - 1)
            grid = tile_grid(field[row_safe, col_safe], block_coords[row_safe, col_safe], block_counts[row_safe, col_safe])
            pieces.append(jnp.where(inside, grid, jnp.zeros((), jnp.float32)))
        strips.append(jnp.concatenate(pieces, axis=1))
    whole = jnp.concatenate(strips, axis=0)
    return jnp.pad(whole[7:17, 7:17], ((0, 0), (0, 0), (1, 1), (0, 0)))

def columns(padded, slot_blocks):
    chan_width = padded.shape[3]
    start_x = slot_blocks // (2 * SLAB_BLOCKS)
    start_y = slot_blocks // SLAB_BLOCKS % 2
    start_z = slot_blocks % SLAB_BLOCKS

    def cut_cube(block_x, block_y, block_z):
        return lax.dynamic_slice(padded, (4 * block_x, 4 * block_y, 4 * block_z, block_x * 0), (6, 6, 6, chan_width))
    cubes = jax.vmap(cut_cube)(start_x, start_y, start_z)
    tap_list = []
    for tap_index in range(27):
        shift_x = tap_index // 9
        shift_y = tap_index // 3 % 3
        shift_z = tap_index % 3
        piece = cubes[:, shift_x:shift_x + 4, shift_y:shift_y + 4, shift_z:shift_z + 4, :]
        tap_list.append(piece.reshape(-1, chan_width))
    return jnp.concatenate(tap_list, axis=1)

def transposed(cols, weight):
    chan_width = weight.shape[1]
    stacked = cols.reshape(cols.shape[0], 27, chan_width).astype(jnp.float32)
    flipped = weight.reshape(27, chan_width, chan_width)[::-1].astype(jnp.float32)
    return jnp.einsum('rkc,kic->ri', stacked, flipped)

def reference(features, block_coords, block_counts, first_weight, second_weight, cotangent):
    tile_total = TILE_ROWS * TILE_COLS
    tile_ids = jnp.arange(tile_total, dtype=jnp.int32)
    grad_scale = 1.0 / math.sqrt(64 * MAX_BLOCKS * tile_total)

    def tile_columns(field, tile):
        tile_row = tile // TILE_COLS
        tile_col = tile % TILE_COLS
        padded = padded_tile(field, block_coords, block_counts, tile_row, tile_col)
        return columns(padded, block_coords[tile_row, tile_col]).astype(jnp.bfloat16)

    def row_live_of(tile):
        live_count = block_counts[tile // TILE_COLS, tile % TILE_COLS]
        return jnp.repeat(jnp.arange(MAX_BLOCKS, dtype=jnp.int32) < live_count, 64)[:, None]

    def rows_of(field, tile):
        return field[tile // TILE_COLS, tile % TILE_COLS].reshape(64 * MAX_BLOCKS, C)

    def forward_hidden(tile):
        pre_first = jnp.dot(tile_columns(features, tile), first_weight, preferred_element_type=jnp.float32)
        return jnp.where(row_live_of(tile), jax.nn.silu(pre_first), jnp.zeros((), jnp.float32)).astype(jnp.bfloat16)
    hidden_all = lax.map(forward_hidden, tile_ids).reshape(features.shape)

    def second_pass(grad_total, tile):
        row_live = row_live_of(tile)
        feature_cols = tile_columns(features, tile)
        pre_first = jnp.dot(feature_cols, first_weight, preferred_element_type=jnp.float32)
        hidden_cols = tile_columns(hidden_all, tile)
        output_rows = jnp.where(row_live, jnp.dot(hidden_cols, second_weight, preferred_element_type=jnp.float32), jnp.zeros((), jnp.float32))
        seed_rows = jnp.where(row_live, rows_of(cotangent, tile).astype(jnp.float32), jnp.zeros((), jnp.float32)).astype(jnp.bfloat16)
        grad_total = grad_total + jnp.dot(hidden_cols.T, seed_rows, preferred_element_type=jnp.float32)
        hidden_grad = transposed(tile_columns(cotangent, tile), second_weight)
        sigmoid_pre = jax.nn.sigmoid(pre_first)
        pre_grad = jnp.where(row_live, hidden_grad * sigmoid_pre * (1.0 + pre_first * (1.0 - sigmoid_pre)), jnp.zeros((), jnp.float32)).astype(jnp.bfloat16)
        return (grad_total, (output_rows, pre_grad))
    second_total, (output_all, pre_grad_all) = lax.scan(second_pass, jnp.zeros((27 * C, C), jnp.float32), tile_ids)
    pre_grad_all = pre_grad_all.reshape(features.shape)

    def third_pass(grad_total, tile):
        row_live = row_live_of(tile)
        feature_cols = tile_columns(features, tile)
        grad_total = grad_total + jnp.dot(feature_cols.T, rows_of(pre_grad_all, tile), preferred_element_type=jnp.float32)
        input_rows = jnp.where(row_live, transposed(tile_columns(pre_grad_all, tile), first_weight), jnp.zeros((), jnp.float32))
        return (grad_total, input_rows)
    first_total, input_all = lax.scan(third_pass, jnp.zeros((27 * C, C), jnp.float32), tile_ids)
    return (output_all.reshape(features.shape), input_all.reshape(features.shape), first_total * grad_scale, second_total * grad_scale)
```

```python
import functools
import math

import jax
import jax.numpy as jnp
import numpy as np
from jax import lax
from jax.experimental import pallas as pl
from jax.experimental.pallas import tpu as pltpu
from jax.sharding import PartitionSpec as P

C = 256
SLOTS = 3
ROWS = 192
FACE = 256
DATA = FACE + ROWS
DEAD = -(1 << 24)
MESH = pl.DeviceIdType.MESH
F32 = jnp.float32
BF16 = jnp.bfloat16

REGIONS = (
    (-1, 0, 0, 48),
    (1, 0, 48, 48),
    (0, -1, 96, 48),
    (0, 1, 144, 48),
    (-1, -1, 192, 16),
    (-1, 1, 208, 16),
    (1, -1, 224, 16),
    (1, 1, 240, 16),
)


def face_tables():
    source = np.full(FACE, -1, np.int64)
    table = np.zeros((8, FACE), np.int32)
    table[1] = DEAD
    for sx, sy, start, _ in REGIONS:
        xs = range(4) if sx == 0 else ((3,) if sx < 0 else (0,))
        ys = range(4) if sy == 0 else ((3,) if sy < 0 else (0,))
        row = start
        for slot in range(SLOTS):
            for vx in xs:
                for vy in ys:
                    for vz in range(4):
                        source[row] = slot * 64 + vx * 16 + vy * 4 + vz
                        table[0, row] = slot
                        table[1, row] = (
                            (8 * sx + vx + 1) * 4096 + (8 * sy + vy + 1) * 64 + vz + 1
                        )
                        row += 1
        table[2, start : start + (48 if sx * sy == 0 else 16)] = -sx
        table[3, start : start + (48 if sx * sy == 0 else 16)] = -sy
    for index, (_, _, start, count) in enumerate(REGIONS):
        table[4, start : start + count] = index
    pick = (source[:, None] == np.arange(ROWS)[None, :]).astype(np.float32)
    return pick, table


def block_codes(coords_ref, counts_ref):
    codes = []
    for slot in range(SLOTS):
        p = coords_ref[0, slot]
        code = (p // 16) * (4 * 4096) + ((p // 8) % 2) * (4 * 64) + (p % 8) * 4
        codes.append((code, slot < counts_ref[0, 0]))
    return codes


def by_slot(slot, codes):
    values = [jnp.where(live, code, DEAD) for code, live in codes]
    return jnp.where(slot == 0, values[0], jnp.where(slot == 1, values[1], values[2]))


def swap_faces(packed, landed, send_sems, recv_sems, extra=()):
    nx, ny = lax.axis_size("gx"), lax.axis_size("gy")
    gx, gy = lax.axis_index("gx"), lax.axis_index("gy")
    copies = []
    for index, (sx, sy, start, count) in enumerate(REGIONS):
        peer = (lax.rem(gx - sx + nx, nx), lax.rem(gy - sy + ny, ny))
        copies.append(
            pltpu.make_async_remote_copy(
                src_ref=packed.at[:, pl.ds(start, count), :],
                dst_ref=landed.at[:, pl.ds(start, count), :],
                send_sem=send_sems.at[index],
                recv_sem=recv_sems.at[index],
                device_id=peer,
                device_id_type=MESH,
            )
        )
        for source, target, sends, recvs in extra:
            copies.append(
                pltpu.make_async_remote_copy(
                    src_ref=source,
                    dst_ref=target.at[index],
                    send_sem=sends.at[index],
                    recv_sem=recvs.at[index],
                    device_id=peer,
                    device_id_type=MESH,
                )
            )
    return copies


def greet_around():
    nx, ny = lax.axis_size("gx"), lax.axis_size("gy")
    gx, gy = lax.axis_index("gx"), lax.axis_index("gy")
    barrier = pltpu.get_barrier_semaphore()
    for sx, sy, _, _ in REGIONS:
        peer = (lax.rem(gx - sx + nx, nx), lax.rem(gy - sy + ny, ny))
        pl.semaphore_signal(barrier, inc=1, device_id=peer, device_id_type=MESH)
    pl.semaphore_wait(barrier, 8)


def first_swap_kernel(
    feat_ref,
    cot_ref,
    pick_ref,
    table_ref,
    coords_ref,
    counts_ref,
    landed_out,
    code_out,
    packed,
    code,
    landed,
    codes_in,
    send_sems,
    recv_sems,
    code_send,
    code_recv,
):
    nx, ny = lax.axis_size("gx"), lax.axis_size("gy")
    gx, gy = lax.axis_index("gx"), lax.axis_index("gy")
    pick = pick_ref[...]
    packed[0] = jnp.dot(pick, feat_ref[...], preferred_element_type=F32).astype(BF16)
    packed[1] = jnp.dot(pick, cot_ref[...], preferred_element_type=F32).astype(BF16)
    blocks = block_codes(coords_ref, counts_ref)
    to_x = gx + table_ref[2:3, :]
    to_y = gy + table_ref[3:4, :]
    inside = (to_x >= 0) & (to_x < nx) & (to_y >= 0) & (to_y < ny)
    sent = table_ref[1:2, :] + by_slot(table_ref[0:1, :], blocks)
    code[...] = jnp.broadcast_to(jnp.where(inside, sent, DEAD), (8, FACE))
    greet_around()
    copies = swap_faces(
        packed, landed, send_sems, recv_sems, ((code, codes_in, code_send, code_recv),)
    )
    for copy in copies:
        copy.start()
    lane = lax.broadcasted_iota(jnp.int32, (8, ROWS), 1)
    voxel = lane % 64
    own = (voxel // 16 + 1) * 4096 + ((voxel // 4) % 4 + 1) * 64 + voxel % 4 + 1
    code_out[:, FACE:] = own + by_slot(lane // 64, blocks)
    for copy in copies:
        copy.wait()
    landed_out[...] = landed[...]
    region = jnp.broadcast_to(table_ref[4:5, :], (8, FACE))
    got = codes_in[0]
    for index in range(1, 8):
        got = jnp.where(region == index, codes_in[index], got)
    code_out[:, :FACE] = got


def second_swap_kernel(packed, landed_out, landed, send_sems, recv_sems):
    greet_around()
    copies = swap_faces(packed, landed, send_sems, recv_sems)
    for copy in copies:
        copy.start()
    for copy in copies:
        copy.wait()
    landed_out[...] = landed[...]


def build_windows(first, second, code_ref, coords_ref, win_ref):
    row = lax.broadcasted_iota(jnp.int32, (96, DATA), 0)
    pattern = (row // 16) * 4096 + ((row // 4) % 4) * 64 + row % 4
    offset = jnp.broadcast_to(code_ref[0:1, :], (96, DATA)) - pattern
    both = jnp.concatenate([first, second], axis=1)
    starts = []
    for slot in range(SLOTS):
        p = coords_ref[0, slot]
        starts.append((p // 16) * (4 * 4096) + ((p // 8) % 2) * (4 * 64) + (p % 8) * 4)
    for shift in range(9):
        placing = jnp.concatenate(
            [
                jnp.where(
                    offset == starts[slot] + (shift // 3) * 64 + shift % 3, 1.0, 0.0
                ).astype(BF16)
                for slot in range(SLOTS)
            ],
            axis=0,
        )
        rows = jnp.dot(placing, both, preferred_element_type=F32).astype(BF16)
        win_ref[0, shift] = rows[:, :C].reshape(SLOTS, 6, 16, C)
        win_ref[1, shift] = rows[:, C:].reshape(SLOTS, 6, 16, C)


def tap_rows(win_ref, field, tap):
    return win_ref[field, tap % 9, :, tap // 9 : tap // 9 + 4].reshape(ROWS, C)


def conv(win_ref, field, weight_ref):
    total = jnp.zeros((ROWS, C), F32)
    for tap in range(27):
        total += jnp.dot(
            tap_rows(win_ref, field, tap),
            weight_ref[tap * C : (tap + 1) * C, :],
            preferred_element_type=F32,
        )
    return total


def conv_back(win_ref, field, weight_ref):
    total = jnp.zeros((ROWS, C), F32)
    for tap in range(27):
        total += lax.dot_general(
            tap_rows(win_ref, field, 26 - tap),
            weight_ref[tap * C : (tap + 1) * C, :],
            (((1,), (1,)), ((), ())),
            preferred_element_type=F32,
        )
    return total


def live_rows(counts_ref):
    return lax.broadcasted_iota(jnp.int32, (ROWS, C), 0) < counts_ref[0, 0] * 64


def middle_kernel(
    feat_ref,
    cot_ref,
    landed_ref,
    code_ref,
    pick_ref,
    coords_ref,
    counts_ref,
    w1_hbm,
    w2_hbm,
    rows_out,
    packed_out,
    seed_win_out,
    win,
    w1,
    w2,
    sems,
):
    loads = [
        pltpu.make_async_copy(w1_hbm, w1, sems.at[0]),
        pltpu.make_async_copy(w2_hbm, w2, sems.at[1]),
    ]
    for load in loads:
        load.start()
    build_windows(
        jnp.concatenate([landed_ref[0], feat_ref[...]], axis=0),
        jnp.concatenate([landed_ref[1], cot_ref[...]], axis=0),
        code_ref,
        coords_ref,
        win,
    )
    live = live_rows(counts_ref)
    loads[0].wait()
    pre = conv(win, 0, w1)
    gate = jax.nn.sigmoid(pre)
    hidden = jnp.where(live, pre * gate, 0.0).astype(BF16)
    loads[1].wait()
    hidden_grad = conv_back(win, 1, w2)
    pre_grad = jnp.where(live, hidden_grad * gate * (1.0 + pre * (1.0 - gate)), 0.0).astype(BF16)
    rows_out[0] = hidden
    rows_out[1] = pre_grad
    pick = pick_ref[...]
    packed_out[0] = jnp.dot(pick, hidden, preferred_element_type=F32).astype(BF16)
    packed_out[1] = jnp.dot(pick, pre_grad, preferred_element_type=F32).astype(BF16)
    seed_win_out[...] = win[1]


def last_kernel(
    scale,
    rows_ref,
    landed_ref,
    code_ref,
    feat_ref,
    seed_win,
    coords_ref,
    counts_ref,
    w1_hbm,
    w2_hbm,
    out_ref,
    grad_ref,
    term1_ref,
    term2_ref,
    win,
    w1,
    w2,
    sems,
):
    loads = [
        pltpu.make_async_copy(w1_hbm, w1, sems.at[0]),
        pltpu.make_async_copy(w2_hbm, w2, sems.at[1]),
    ]
    for load in loads:
        load.start()
    build_windows(
        jnp.concatenate([landed_ref[0], rows_ref[0]], axis=0),
        jnp.concatenate([landed_ref[1], rows_ref[1]], axis=0),
        code_ref,
        coords_ref,
        win,
    )
    live = live_rows(counts_ref)
    feat = jnp.where(live, feat_ref[...].astype(F32), 0.0).T.astype(BF16)
    hidden = rows_ref[0].astype(F32).T.astype(BF16)
    for tap in range(27):
        back = 26 - tap
        place = pl.ds(tap * C, C)
        term1_ref[place, :] = scale * jnp.dot(
            feat, tap_rows(win, 1, back), preferred_element_type=F32
        )
        seed = seed_win[back % 9, :, back // 9 : back // 9 + 4].reshape(ROWS, C)
        term2_ref[place, :] = scale * jnp.dot(hidden, seed, preferred_element_type=F32)
    for load in loads:
        load.wait()
    out_ref[...] = jnp.where(live, conv(win, 0, w2), 0.0)
    grad_ref[...] = jnp.where(live, conv_back(win, 1, w1), 0.0)


def vmem():
    return pl.BlockSpec(memory_space=pltpu.VMEM)


def smem():
    return pl.BlockSpec(memory_space=pltpu.SMEM)


def hbm():
    return pl.BlockSpec(memory_space=pl.ANY)


def reduce_weights(term):
    narrowed = lax.psum_scatter(term, "gx", scatter_dimension=0, tiled=True)
    return lax.psum_scatter(narrowed, "gy", scatter_dimension=1, tiled=True)


def per_device(features, block_coords, block_counts, first_weight, second_weight, cotangent):
    feat = features.reshape(ROWS, C)
    cot = cotangent.reshape(ROWS, C)
    coords = block_coords.reshape(1, SLOTS)
    counts = block_counts.reshape(1, 1)
    pick_np, table_np = face_tables()
    pick = jnp.asarray(pick_np, BF16)
    table = jnp.asarray(table_np)
    struct = jax.ShapeDtypeStruct
    scale = 1.0 / math.sqrt(64 * SLOTS * lax.axis_size("gx") * lax.axis_size("gy"))
    landed, code = pl.pallas_call(
        first_swap_kernel,
        out_shape=(struct((2, FACE, C), BF16), struct((8, DATA), jnp.int32)),
        in_specs=[vmem()] * 4 + [smem()] * 2,
        out_specs=(vmem(), vmem()),
        scratch_shapes=[
            pltpu.VMEM((2, FACE, C), BF16),
            pltpu.VMEM((8, FACE), jnp.int32),
            pltpu.VMEM((2, FACE, C), BF16),
            pltpu.VMEM((8, 8, FACE), jnp.int32),
        ]
        + [pltpu.SemaphoreType.DMA((8,))] * 4,
        compiler_params=pltpu.CompilerParams(collective_id=0, has_side_effects=True),
        name="first_swap",
    )(feat, cot, pick, table, coords, counts)
    weights = [pltpu.VMEM((27 * C, C), BF16)] * 2 + [pltpu.SemaphoreType.DMA((2,))]
    window = (9, SLOTS, 6, 16, C)
    rows, packed, seed_win = pl.pallas_call(
        middle_kernel,
        out_shape=(
            struct((2, ROWS, C), BF16),
            struct((2, FACE, C), BF16),
            struct(window, BF16),
        ),
        in_specs=[vmem()] * 5 + [smem()] * 2 + [hbm()] * 2,
        out_specs=(vmem(), vmem(), vmem()),
        scratch_shapes=[pltpu.VMEM((2,) + window, BF16)] + weights,
        compiler_params=pltpu.CompilerParams(vmem_limit_bytes=40 << 20),
        name="middle",
    )(feat, cot, landed, code, pick, coords, counts, first_weight, second_weight)
    landed2 = pl.pallas_call(
        second_swap_kernel,
        out_shape=struct((2, FACE, C), BF16),
        in_specs=[vmem()],
        out_specs=vmem(),
        scratch_shapes=[pltpu.VMEM((2, FACE, C), BF16)] + [pltpu.SemaphoreType.DMA((8,))] * 2,
        compiler_params=pltpu.CompilerParams(collective_id=1, has_side_effects=True),
        name="second_swap",
    )(packed)
    out, grad, term1, term2 = pl.pallas_call(
        functools.partial(last_kernel, scale),
        out_shape=(
            struct((ROWS, C), F32),
            struct((ROWS, C), F32),
            struct((27 * C, C), F32),
            struct((27 * C, C), F32),
        ),
        in_specs=[vmem()] * 5 + [smem()] * 2 + [hbm()] * 2,
        out_specs=(vmem(),) * 4,
        scratch_shapes=[pltpu.VMEM((2,) + window, BF16)] + weights,
        compiler_params=pltpu.CompilerParams(vmem_limit_bytes=56 << 20),
        name="last",
    )(rows, landed2, code, feat, seed_win, coords, counts, first_weight, second_weight)
    return (
        out.reshape(features.shape),
        grad.reshape(features.shape),
        reduce_weights(term1),
        reduce_weights(term2),
    )


def solution(mesh):
    placed = (
        P("gx", "gy", None, None, None),
        P("gx", "gy", None),
        P("gx", "gy"),
        P(),
        P(),
        P("gx", "gy", None, None, None),
    )
    return jax.shard_map(
        per_device,
        mesh=mesh,
        in_specs=placed,
        out_specs=(
            P("gx", "gy", None, None, None),
            P("gx", "gy", None, None, None),
            P("gx", "gy"),
            P("gx", "gy"),
        ),
        check_vma=False,
    )
```

```python
import functools
import math

import jax
import jax.numpy as jnp
import numpy as np
from jax import lax
from jax.experimental import pallas as pl
from jax.experimental.pallas import tpu as pltpu
from jax.sharding import PartitionSpec as P

C = 256
SLOTS = 3
ROWS = 192
FACE = 256
DATA = FACE + ROWS
DEAD = -(1 << 24)
MESH = pl.DeviceIdType.MESH
F32 = jnp.float32
BF16 = jnp.bfloat16

REGIONS = (
    (-1, 0, 0, 48),
    (1, 0, 48, 48),
    (0, -1, 96, 48),
    (0, 1, 144, 48),
    (-1, -1, 192, 16),
    (-1, 1, 208, 16),
    (1, -1, 224, 16),
    (1, 1, 240, 16),
)


def face_tables():
    source = np.full(FACE, -1, np.int64)
    table = np.zeros((8, FACE), np.int32)
    table[1] = DEAD
    for sx, sy, start, _ in REGIONS:
        xs = range(4) if sx == 0 else ((3,) if sx < 0 else (0,))
        ys = range(4) if sy == 0 else ((3,) if sy < 0 else (0,))
        row = start
        for slot in range(SLOTS):
            for vx in xs:
                for vy in ys:
                    for vz in range(4):
                        source[row] = slot * 64 + vx * 16 + vy * 4 + vz
                        table[0, row] = slot
                        table[1, row] = (
                            (8 * sx + vx + 1) * 4096 + (8 * sy + vy + 1) * 64 + vz + 1
                        )
                        row += 1
        table[2, start : start + (48 if sx * sy == 0 else 16)] = -sx
        table[3, start : start + (48 if sx * sy == 0 else 16)] = -sy
    for index, (_, _, start, count) in enumerate(REGIONS):
        table[4, start : start + count] = index
    pick = (source[:, None] == np.arange(ROWS)[None, :]).astype(np.float32)
    return pick, table


def block_codes(coords_ref, counts_ref):
    codes = []
    for slot in range(SLOTS):
        p = coords_ref[0, slot]
        code = (p // 16) * (4 * 4096) + ((p // 8) % 2) * (4 * 64) + (p % 8) * 4
        codes.append((code, slot < counts_ref[0, 0]))
    return codes


def by_slot(slot, codes):
    values = [jnp.where(live, code, DEAD) for code, live in codes]
    return jnp.where(slot == 0, values[0], jnp.where(slot == 1, values[1], values[2]))


def swap_faces(packed, landed, send_sems, recv_sems, extra=()):
    nx, ny = lax.axis_size("gx"), lax.axis_size("gy")
    gx, gy = lax.axis_index("gx"), lax.axis_index("gy")
    copies = []
    for index, (sx, sy, start, count) in enumerate(REGIONS):
        peer = (lax.rem(gx - sx + nx, nx), lax.rem(gy - sy + ny, ny))
        copies.append(
            pltpu.make_async_remote_copy(
                src_ref=packed.at[:, pl.ds(start, count), :],
                dst_ref=landed.at[:, pl.ds(start, count), :],
                send_sem=send_sems.at[index],
                recv_sem=recv_sems.at[index],
                device_id=peer,
                device_id_type=MESH,
            )
        )
        for source, target, sends, recvs in extra:
            copies.append(
                pltpu.make_async_remote_copy(
                    src_ref=source,
                    dst_ref=target.at[index],
                    send_sem=sends.at[index],
                    recv_sem=recvs.at[index],
                    device_id=peer,
                    device_id_type=MESH,
                )
            )
    return copies


def around():
    nx, ny = lax.axis_size("gx"), lax.axis_size("gy")
    gx, gy = lax.axis_index("gx"), lax.axis_index("gy")
    return [
        (lax.rem(gx - sx + nx, nx), lax.rem(gy - sy + ny, ny)) for sx, sy, _, _ in REGIONS
    ]


def greet(peers):
    barrier = pltpu.get_barrier_semaphore()
    for peer in peers:
        pl.semaphore_signal(barrier, inc=1, device_id=peer, device_id_type=MESH)
    pl.semaphore_wait(barrier, len(peers))


def first_swap_kernel(
    feat_ref,
    cot_ref,
    pick_ref,
    table_ref,
    coords_ref,
    counts_ref,
    landed_out,
    code_out,
    packed,
    code,
    landed,
    codes_in,
    send_sems,
    recv_sems,
    code_send,
    code_recv,
):
    nx, ny = lax.axis_size("gx"), lax.axis_size("gy")
    gx, gy = lax.axis_index("gx"), lax.axis_index("gy")
    pick = pick_ref[...]
    packed[0] = jnp.dot(pick, feat_ref[...], preferred_element_type=F32).astype(BF16)
    packed[1] = jnp.dot(pick, cot_ref[...], preferred_element_type=F32).astype(BF16)
    blocks = block_codes(coords_ref, counts_ref)
    to_x = gx + table_ref[2:3, :]
    to_y = gy + table_ref[3:4, :]
    inside = (to_x >= 0) & (to_x < nx) & (to_y >= 0) & (to_y < ny)
    sent = table_ref[1:2, :] + by_slot(table_ref[0:1, :], blocks)
    code[...] = jnp.broadcast_to(jnp.where(inside, sent, DEAD), (8, FACE))
    greet(around())
    copies = swap_faces(
        packed, landed, send_sems, recv_sems, ((code, codes_in, code_send, code_recv),)
    )
    for copy in copies:
        copy.start()
    lane = lax.broadcasted_iota(jnp.int32, (8, ROWS), 1)
    voxel = lane % 64
    own = (voxel // 16 + 1) * 4096 + ((voxel // 4) % 4 + 1) * 64 + voxel % 4 + 1
    code_out[:, FACE:] = own + by_slot(lane // 64, blocks)
    for copy in copies:
        copy.wait()
    landed_out[...] = landed[...]
    region = jnp.broadcast_to(table_ref[4:5, :], (8, FACE))
    got = codes_in[0]
    for index in range(1, 8):
        got = jnp.where(region == index, codes_in[index], got)
    code_out[:, :FACE] = got


def build_windows(first, second, code_ref, coords_ref, win_ref):
    row = lax.broadcasted_iota(jnp.int32, (96, DATA), 0)
    pattern = (row // 16) * 4096 + ((row // 4) % 4) * 64 + row % 4
    offset = jnp.broadcast_to(code_ref[0:1, :], (96, DATA)) - pattern
    both = jnp.concatenate([first, second], axis=1)
    starts = []
    for slot in range(SLOTS):
        p = coords_ref[0, slot]
        starts.append((p // 16) * (4 * 4096) + ((p // 8) % 2) * (4 * 64) + (p % 8) * 4)
    for shift in range(9):
        placing = jnp.concatenate(
            [
                jnp.where(
                    offset == starts[slot] + (shift // 3) * 64 + shift % 3, 1.0, 0.0
                ).astype(BF16)
                for slot in range(SLOTS)
            ],
            axis=0,
        )
        rows = jnp.dot(placing, both, preferred_element_type=F32).astype(BF16)
        win_ref[0, shift] = rows[:, :C].reshape(SLOTS, 6, 16, C)
        win_ref[1, shift] = rows[:, C:].reshape(SLOTS, 6, 16, C)


def tap_rows(win_ref, field, tap):
    return win_ref[field, tap % 9, :, tap // 9 : tap // 9 + 4].reshape(ROWS, C)


def conv(win_ref, field, weight_ref):
    total = jnp.zeros((ROWS, C), F32)
    for tap in range(27):
        total += jnp.dot(
            tap_rows(win_ref, field, tap),
            weight_ref[tap * C : (tap + 1) * C, :],
            preferred_element_type=F32,
        )
    return total


def conv_back(win_ref, field, weight_ref):
    total = jnp.zeros((ROWS, C), F32)
    for tap in range(27):
        total += lax.dot_general(
            tap_rows(win_ref, field, 26 - tap),
            weight_ref[tap * C : (tap + 1) * C, :],
            (((1,), (1,)), ((), ())),
            preferred_element_type=F32,
        )
    return total


def live_rows(counts_ref):
    return lax.broadcasted_iota(jnp.int32, (ROWS, C), 0) < counts_ref[0, 0] * 64


def middle_kernel(
    feat_ref,
    cot_ref,
    landed_ref,
    code_ref,
    pick_ref,
    coords_ref,
    counts_ref,
    w1_hbm,
    w2_hbm,
    rows_out,
    packed_out,
    win,
    w1,
    w2,
    sems,
):
    loads = [
        pltpu.make_async_copy(w1_hbm, w1, sems.at[0]),
        pltpu.make_async_copy(w2_hbm, w2, sems.at[1]),
    ]
    for load in loads:
        load.start()
    build_windows(
        jnp.concatenate([landed_ref[0], feat_ref[...]], axis=0),
        jnp.concatenate([landed_ref[1], cot_ref[...]], axis=0),
        code_ref,
        coords_ref,
        win,
    )
    live = live_rows(counts_ref)
    loads[0].wait()
    pre = conv(win, 0, w1)
    gate = jax.nn.sigmoid(pre)
    hidden = jnp.where(live, pre * gate, 0.0).astype(BF16)
    loads[1].wait()
    hidden_grad = conv_back(win, 1, w2)
    pre_grad = jnp.where(live, hidden_grad * gate * (1.0 + pre * (1.0 - gate)), 0.0).astype(BF16)
    rows_out[0] = hidden
    rows_out[1] = pre_grad
    pick = pick_ref[...]
    packed_out[0] = jnp.dot(pick, hidden, preferred_element_type=F32).astype(BF16)
    packed_out[1] = jnp.dot(pick, pre_grad, preferred_element_type=F32).astype(BF16)


def last_kernel(
    rows_ref,
    landed_ref,
    code_ref,
    coords_ref,
    counts_ref,
    w1_hbm,
    w2_hbm,
    out_ref,
    grad_ref,
    win,
    w1,
    w2,
    sems,
):
    loads = [
        pltpu.make_async_copy(w1_hbm, w1, sems.at[0]),
        pltpu.make_async_copy(w2_hbm, w2, sems.at[1]),
    ]
    for load in loads:
        load.start()
    build_windows(
        jnp.concatenate([landed_ref[0], rows_ref[0]], axis=0),
        jnp.concatenate([landed_ref[1], rows_ref[1]], axis=0),
        code_ref,
        coords_ref,
        win,
    )
    live = live_rows(counts_ref)
    for load in loads:
        load.wait()
    out_ref[...] = jnp.where(live, conv(win, 0, w2), 0.0)
    grad_ref[...] = jnp.where(live, conv_back(win, 1, w1), 0.0)


BLOCK = 216
TILES = 27
PACKED = 56


class Ring:
    def __init__(self, own, out, inbox, sends, recvs, me, right, left, place):
        self.own, self.out, self.inbox = own, out, inbox
        self.me = place(me)
        self.to_right = place(lax.rem(me + 1, 4))
        self.to_left = place(lax.rem(me + 3, 4))
        across = place(lax.rem(me + 2, 4))
        self.half = own.shape[1] // 2
        low, high = pl.ds(0, self.half), pl.ds(self.half, self.half)
        plan = (
            (across, high, right),
            (across, low, left),
            (self.to_right, low, right),
            (self.to_left, high, left),
            (self.to_right, high, right),
            (self.to_left, low, left),
        )
        self.copies = [
            pltpu.make_async_remote_copy(
                src_ref=out.at[target, part],
                dst_ref=inbox.at[index],
                send_sem=sends.at[index],
                recv_sem=recvs.at[index],
                device_id=peer,
                device_id_type=MESH,
            )
            for index, (target, part, peer) in enumerate(plan)
        ]

    def start(self):
        for copy in self.copies[:4]:
            copy.start()

    def relay(self):
        half = self.half
        for index, target, base in ((0, self.to_right, half), (1, self.to_left, 0)):
            self.copies[index].wait_recv()

            @pl.loop(0, half)
            def _(z):
                total = self.own[target, base + z] + self.inbox[index, z].astype(F32)
                self.out[target, base + z] = total.astype(BF16)

            self.copies[4 + index].start()

    def arrive(self):
        for copy in self.copies[2:]:
            copy.wait_recv()

    def total(self, z, upper):
        first, second = (3, 4) if upper else (2, 5)
        mine = self.own[self.me, z + self.half if upper else z]
        return mine + self.inbox[first, z].astype(F32) + self.inbox[second, z].astype(F32)

    def drain(self):
        for copy in self.copies:
            copy.wait_send()


def ring_scratch(nz, rows):
    return [
        pltpu.VMEM((4, nz, rows, 128), F32),
        pltpu.VMEM((4, nz, rows, 128), BF16),
        pltpu.VMEM((6, nz // 2, rows, 128), BF16),
        pltpu.SemaphoreType.DMA((6,)),
        pltpu.SemaphoreType.DMA((6,)),
    ]


def reduce_scratch(nz):
    return (
        ring_scratch(nz, BLOCK) * 2
        + ring_scratch(nz, PACKED) * 2
        + [
            pltpu.VMEM((2, nz, PACKED, 128), F32),
            pltpu.VMEM((2, nz, PACKED, 128), F32),
            pltpu.VMEM((2, PACKED, 128), F32),
            pltpu.VMEM((PACKED, 128), F32),
            pltpu.SemaphoreType.DMA((2, nz)),
            pltpu.SemaphoreType.DMA((2, nz)),
            pltpu.SemaphoreType.DMA((2,)),
        ]
    )


def swapped(t):
    return lax.rem(t, 2) * 2 + t // 2


def straight(t):
    return t


def chip_place():
    gx, gy = lax.axis_index("gx"), lax.axis_index("gy")
    z, x, core, y = gx // 4, (lax.rem(gx, 4) // 2) * 2 + lax.rem(gy, 2), lax.rem(gx, 2), gy // 2
    return x, y, z, core


def device_at(x, y, z, core):
    return (z * 4 + (x // 2) * 2 + core, y * 2 + lax.rem(x, 2))


def reduce_peers(nz):
    x, y, z, core = chip_place()
    return (
        [device_at(x, y, z, 1 - core)]
        + [device_at(lax.rem(x + step, 4), y, z, core) for step in (1, 3)]
        + [device_at(x, lax.rem(y + step, 4), z, core) for step in (1, 3)]
        + [device_at(x, y, lax.rem(z + step, nz), core) for step in range(1, nz)]
    )


def spread(rows, own, out, z):
    lane = lax.broadcasted_iota(jnp.int32, (8, 128), 1) // 32
    tiles = rows.reshape(TILES, 8, 128)
    for target in range(4):
        packed = []
        for group in range(7):
            tile = None
            for part in range(4):
                index = 4 * group + part
                if index >= TILES:
                    continue
                shift = (part - target) % 4 * 32
                moved = pltpu.roll(tiles[index], shift, 1) if shift else tiles[index]
                tile = moved if tile is None else jnp.where(lane == part, moved, tile)
            packed.append(tile)
        block = jnp.concatenate(packed, axis=0)
        own[target, z] = block
        out[target, z] = block.astype(BF16)


def unspread(packed, target_ref):
    tiles = packed.reshape(7, 8, 128)
    for index in range(TILES):
        tile = tiles[index // 4]
        part = index % 4
        moved = pltpu.roll(tile, 128 - 32 * part, 1) if part else tile
        target_ref[index * 8 : index * 8 + 8, :] = moved[:, :32]


def reduce_terms(nz, scale, term, first_ref, second_ref, scratch):
    x, y, z, core = chip_place()
    xs, ys, ys2, xs2 = (scratch[5 * i : 5 * i + 5] for i in range(4))
    zown, zin, last, got, zsend, zrecv, psem = scratch[20:]
    x_right = device_at(lax.rem(x + 1, 4), y, z, core)
    x_left = device_at(lax.rem(x + 3, 4), y, z, core)
    y_right = device_at(x, lax.rem(y + 1, 4), z, core)
    y_left = device_at(x, lax.rem(y + 3, 4), z, core)
    partner = device_at(x, y, z, 1 - core)
    firsts = [
        Ring(*xs, x, x_right, x_left, straight),
        Ring(*ys, y, y_right, y_left, straight),
    ]
    seconds = [
        Ring(*ys2, y, y_right, y_left, swapped),
        Ring(*xs2, x, x_right, x_left, straight),
    ]
    lane = lax.broadcasted_iota(jnp.int32, (BLOCK, 128), 1)
    even = (lane // 32) % 2 == 0
    below = lane < 64

    def place(target, index, value):
        own, out = target
        own[index] = value
        out[index] = value.astype(BF16)

    @pl.loop(0, 2 * nz)
    def _(block):
        to_z, to_xh = block // 2, lax.rem(block, 2)
        rows = pl.ds(pl.multiple_of(block * (2 * BLOCK), 8), BLOCK)
        left, right = term[rows, :128], term[rows, 128:]
        place(xs[:2], (2 * to_xh, to_z), jnp.where(even, left, pltpu.roll(right, 32, 1)))
        place(xs[:2], (2 * to_xh + 1, to_z), jnp.where(even, pltpu.roll(left, 96, 1), right))

    firsts[0].start()

    @pl.loop(0, nz)
    def _(to_z):
        rows = [
            pl.ds(pl.multiple_of(to_z * (4 * BLOCK) + (2 * half + 1) * BLOCK, 8), BLOCK)
            for half in range(2)
        ]
        for pair in range(2):
            lanes = slice(128 * pair, 128 * pair + 128)
            zero, one = term[rows[0], lanes], term[rows[1], lanes]
            place(ys[:2], (2 * pair, to_z), jnp.where(below, zero, pltpu.roll(one, 64, 1)))
            place(ys[:2], (2 * pair + 1, to_z), jnp.where(below, pltpu.roll(zero, 64, 1), one))

    firsts[1].start()
    for ring in firsts:
        ring.relay()
    for ring, following in zip(firsts, seconds):
        ring.arrive()
        half = ring.half

        for upper in range(2):

            @pl.loop(0, half)
            def _(index):
                spread(
                    ring.total(index, upper),
                    following.own,
                    following.out,
                    index + upper * half,
                )

        following.start()
    for ring in seconds:
        ring.relay()
    zcopies = []
    for color, ring in enumerate(seconds):
        ring.arrive()
        half = ring.half

        for upper in range(2):

            @pl.loop(0, half)
            def _(index):
                zown[color, index + upper * half] = ring.total(index, upper)

        for step in range(1, nz):
            to_z = lax.rem(z + step, nz)
            copy = pltpu.make_async_remote_copy(
                src_ref=zown.at[color, to_z],
                dst_ref=zin.at[color, step],
                send_sem=zsend.at[color, step],
                recv_sem=zrecv.at[color, step],
                device_id=device_at(x, y, to_z, core),
                device_id_type=MESH,
            )
            copy.start()
            zcopies.append(copy)
    for color in range(2):
        total = zown[color, z]
        for step in range(1, nz):
            zcopies[color * (nz - 1) + step - 1].wait_recv()
            total += zin[color, step]
        last[color] = total * scale
    copy = pltpu.make_async_remote_copy(
        src_ref=last.at[1 - core],
        dst_ref=got,
        send_sem=psem.at[0],
        recv_sem=psem.at[1],
        device_id=partner,
        device_id_type=MESH,
    )
    copy.start()
    for ring in firsts + seconds:
        ring.drain()
    for sent in zcopies:
        sent.wait_send()
    copy.wait()
    mine, other = last[core], got[...]
    first = core == 0
    unspread(jnp.where(first, mine, other), first_ref)
    unspread(jnp.where(first, other, mine), second_ref)


def reduce_kernel(
    nz,
    scale,
    win_ref,
    rows_ref,
    packed,
    landed_out,
    first_ref,
    second_ref,
    landed,
    send_sems,
    recv_sems,
    pair_win,
    pair_rows,
    pair_sems,
    turned,
    term,
    *scratch,
):
    x, y, z, core = chip_place()
    greet(around() + reduce_peers(nz))
    partner = device_at(x, y, z, 1 - core)
    pair = [
        pltpu.make_async_remote_copy(
            src_ref=source,
            dst_ref=target,
            send_sem=pair_sems.at[2 * index],
            recv_sem=pair_sems.at[2 * index + 1],
            device_id=partner,
            device_id_type=MESH,
        )
        for index, (source, target) in enumerate(
            ((win_ref.at[1 - core], pair_win), (rows_ref.at[core], pair_rows))
        )
    ]
    for copy in pair:
        copy.start()
    faces = swap_faces(packed, landed, send_sems, recv_sems)
    for copy in faces:
        copy.start()
    for copy in pair:
        copy.wait()

    def window(tap):
        shift, start = lax.rem(tap, 9), tap // 9
        return jnp.concatenate(
            [
                win_ref[core, shift, :, pl.ds(start, 4)].reshape(ROWS, C),
                pair_win[shift, :, pl.ds(start, 4)].reshape(ROWS, C),
            ],
            axis=0,
        )

    @pl.when(core == 0)
    def _():
        right = jnp.concatenate([rows_ref[1], pair_rows[...]], axis=0)

        @pl.loop(0, 27)
        def _(tap):
            term[pl.ds(pl.multiple_of(tap * C, C), C), :] = lax.dot_general(
                window(tap), right, (((0,), (0,)), ((), ())), preferred_element_type=F32
            )

    @pl.when(core == 1)
    def _():
        both = jnp.concatenate([rows_ref[0], pair_rows[...]], axis=0)
        turned[...] = both.astype(F32).T.astype(BF16)

        @pl.loop(0, 27)
        def _(tap):
            term[pl.ds(pl.multiple_of(tap * C, C), C), :] = jnp.dot(
                turned[...], window(26 - tap), preferred_element_type=F32
            )

    reduce_terms(nz, scale, term, first_ref, second_ref, scratch)
    for copy in faces:
        copy.wait()
    landed_out[...] = landed[...]


def vmem():
    return pl.BlockSpec(memory_space=pltpu.VMEM)


def smem():
    return pl.BlockSpec(memory_space=pltpu.SMEM)


def hbm():
    return pl.BlockSpec(memory_space=pl.ANY)


def per_device(features, block_coords, block_counts, first_weight, second_weight, cotangent):
    feat = features.reshape(ROWS, C)
    cot = cotangent.reshape(ROWS, C)
    coords = block_coords.reshape(1, SLOTS)
    counts = block_counts.reshape(1, 1)
    pick_np, table_np = face_tables()
    pick = jnp.asarray(pick_np, BF16)
    table = jnp.asarray(table_np)
    struct = jax.ShapeDtypeStruct
    scale = 1.0 / math.sqrt(64 * SLOTS * lax.axis_size("gx") * lax.axis_size("gy"))
    landed, code = pl.pallas_call(
        first_swap_kernel,
        out_shape=(struct((2, FACE, C), BF16), struct((8, DATA), jnp.int32)),
        in_specs=[vmem()] * 4 + [smem()] * 2,
        out_specs=(vmem(), vmem()),
        scratch_shapes=[
            pltpu.VMEM((2, FACE, C), BF16),
            pltpu.VMEM((8, FACE), jnp.int32),
            pltpu.VMEM((2, FACE, C), BF16),
            pltpu.VMEM((8, 8, FACE), jnp.int32),
        ]
        + [pltpu.SemaphoreType.DMA((8,))] * 4,
        compiler_params=pltpu.CompilerParams(collective_id=0, has_side_effects=True),
        name="first_swap",
    )(feat, cot, pick, table, coords, counts)
    weights = [pltpu.VMEM((27 * C, C), BF16)] * 2 + [pltpu.SemaphoreType.DMA((2,))]
    window = (9, SLOTS, 6, 16, C)
    rows, packed, win = pl.pallas_call(
        middle_kernel,
        out_shape=(
            struct((2, ROWS, C), BF16),
            struct((2, FACE, C), BF16),
            struct((2,) + window, BF16),
        ),
        in_specs=[vmem()] * 5 + [smem()] * 2 + [hbm()] * 2,
        out_specs=(vmem(), vmem(), vmem()),
        scratch_shapes=weights,
        compiler_params=pltpu.CompilerParams(vmem_limit_bytes=40 << 20),
        name="middle",
    )(feat, cot, landed, code, pick, coords, counts, first_weight, second_weight)
    nz = lax.axis_size("gx") // 4
    landed2, first_grad, second_grad = pl.pallas_call(
        functools.partial(reduce_kernel, nz, scale),
        out_shape=(
            struct((2, FACE, C), BF16),
            struct((BLOCK, 32), F32),
            struct((BLOCK, 32), F32),
        ),
        in_specs=[vmem()] * 3,
        out_specs=(vmem(), vmem(), vmem()),
        scratch_shapes=[
            pltpu.VMEM((2, FACE, C), BF16),
            pltpu.SemaphoreType.DMA((8,)),
            pltpu.SemaphoreType.DMA((8,)),
            pltpu.VMEM(window, BF16),
            pltpu.VMEM((ROWS, C), BF16),
            pltpu.SemaphoreType.DMA((4,)),
            pltpu.VMEM((C, 2 * ROWS), BF16),
            pltpu.VMEM((27 * C, C), F32),
        ]
        + reduce_scratch(nz),
        compiler_params=pltpu.CompilerParams(
            collective_id=1, has_side_effects=True, vmem_limit_bytes=50 << 20
        ),
        name="reduce",
    )(win, rows, packed)
    out, grad = pl.pallas_call(
        last_kernel,
        out_shape=(struct((ROWS, C), F32), struct((ROWS, C), F32)),
        in_specs=[vmem()] * 3 + [smem()] * 2 + [hbm()] * 2,
        out_specs=(vmem(), vmem()),
        scratch_shapes=[pltpu.VMEM((2,) + window, BF16)] + weights,
        compiler_params=pltpu.CompilerParams(vmem_limit_bytes=40 << 20),
        name="last",
    )(rows, landed2, code, coords, counts, first_weight, second_weight)
    return out.reshape(features.shape), grad.reshape(features.shape), first_grad, second_grad


def solution(mesh):
    placed = (
        P("gx", "gy", None, None, None),
        P("gx", "gy", None),
        P("gx", "gy"),
        P(),
        P(),
        P("gx", "gy", None, None, None),
    )
    return jax.shard_map(
        per_device,
        mesh=mesh,
        in_specs=placed,
        out_specs=(
            P("gx", "gy", None, None, None),
            P("gx", "gy", None, None, None),
            P("gx", "gy"),
            P("gx", "gy"),
        ),
        check_vma=False,
    )
```

```python
import functools
import math

import jax
import jax.numpy as jnp
import numpy as np
from jax import lax
from jax.experimental import pallas as pl
from jax.experimental.pallas import tpu as pltpu
from jax.sharding import PartitionSpec as P

C = 256
SLOTS = 3
ROWS = 192
FACE = 256
DATA = FACE + ROWS
DEAD = -(1 << 24)
LIMIT = 56 << 20
MESH = pl.DeviceIdType.MESH
F32 = jnp.float32
BF16 = jnp.bfloat16

REGIONS = (
    (-1, 0, 0, 48),
    (1, 0, 48, 48),
    (0, -1, 96, 48),
    (0, 1, 144, 48),
    (-1, -1, 192, 16),
    (-1, 1, 208, 16),
    (1, -1, 224, 16),
    (1, 1, 240, 16),
)


def face_tables():
    source = np.full(FACE, -1, np.int64)
    table = np.zeros((8, FACE), np.int32)
    table[1] = DEAD
    for sx, sy, start, _ in REGIONS:
        xs = range(4) if sx == 0 else ((3,) if sx < 0 else (0,))
        ys = range(4) if sy == 0 else ((3,) if sy < 0 else (0,))
        row = start
        for slot in range(SLOTS):
            for vx in xs:
                for vy in ys:
                    for vz in range(4):
                        source[row] = slot * 64 + vx * 16 + vy * 4 + vz
                        table[0, row] = slot
                        table[1, row] = (
                            (8 * sx + vx + 1) * 4096 + (8 * sy + vy + 1) * 64 + vz + 1
                        )
                        row += 1
        table[2, start : start + (48 if sx * sy == 0 else 16)] = -sx
        table[3, start : start + (48 if sx * sy == 0 else 16)] = -sy
    for index, (_, _, start, count) in enumerate(REGIONS):
        table[4, start : start + count] = index
    pick = (source[:, None] == np.arange(ROWS)[None, :]).astype(np.float32)
    return pick, table


def block_codes(coords_ref, counts_ref):
    codes = []
    for slot in range(SLOTS):
        p = coords_ref[0, slot]
        code = (p // 16) * (4 * 4096) + ((p // 8) % 2) * (4 * 64) + (p % 8) * 4
        codes.append((code, slot < counts_ref[0, 0]))
    return codes


def by_slot(slot, codes):
    values = [jnp.where(live, code, DEAD) for code, live in codes]
    return jnp.where(slot == 0, values[0], jnp.where(slot == 1, values[1], values[2]))


def swap_faces(packed, landed, send_sems, recv_sems, extra=()):
    nx, ny = lax.axis_size("gx"), lax.axis_size("gy")
    gx, gy = lax.axis_index("gx"), lax.axis_index("gy")
    copies = []
    for index, (sx, sy, start, count) in enumerate(REGIONS):
        peer = (lax.rem(gx - sx + nx, nx), lax.rem(gy - sy + ny, ny))
        copies.append(
            pltpu.make_async_remote_copy(
                src_ref=packed.at[:, pl.ds(start, count), :],
                dst_ref=landed.at[:, pl.ds(start, count), :],
                send_sem=send_sems.at[index],
                recv_sem=recv_sems.at[index],
                device_id=peer,
                device_id_type=MESH,
            )
        )
        for source, target, sends, recvs in extra:
            copies.append(
                pltpu.make_async_remote_copy(
                    src_ref=source,
                    dst_ref=target.at[index],
                    send_sem=sends.at[index],
                    recv_sem=recvs.at[index],
                    device_id=peer,
                    device_id_type=MESH,
                )
            )
    return copies


def around():
    nx, ny = lax.axis_size("gx"), lax.axis_size("gy")
    gx, gy = lax.axis_index("gx"), lax.axis_index("gy")
    return [
        (lax.rem(gx - sx + nx, nx), lax.rem(gy - sy + ny, ny)) for sx, sy, _, _ in REGIONS
    ]


def build_windows(first, second, code_ref, coords_ref, win_ref):
    row = lax.broadcasted_iota(jnp.int32, (96, DATA), 0)
    pattern = (row // 16) * 4096 + ((row // 4) % 4) * 64 + row % 4
    offset = jnp.broadcast_to(code_ref[0:1, :], (96, DATA)) - pattern
    both = jnp.concatenate([first, second], axis=1)
    starts = []
    for slot in range(SLOTS):
        p = coords_ref[0, slot]
        starts.append((p // 16) * (4 * 4096) + ((p // 8) % 2) * (4 * 64) + (p % 8) * 4)
    for shift in range(9):
        placing = jnp.concatenate(
            [
                jnp.where(
                    offset == starts[slot] + (shift // 3) * 64 + shift % 3, 1.0, 0.0
                ).astype(BF16)
                for slot in range(SLOTS)
            ],
            axis=0,
        )
        rows = jnp.dot(placing, both, preferred_element_type=F32).astype(BF16)
        win_ref[0, shift] = rows[:, :C].reshape(SLOTS, 6, 16, C)
        win_ref[1, shift] = rows[:, C:].reshape(SLOTS, 6, 16, C)


def tap_rows(win_ref, field, tap):
    return win_ref[field, tap % 9, :, tap // 9 : tap // 9 + 4].reshape(ROWS, C)


def conv(win_ref, field, weight_ref):
    total = jnp.zeros((ROWS, C), F32)
    for tap in range(27):
        total += jnp.dot(
            tap_rows(win_ref, field, tap),
            weight_ref[tap * C : (tap + 1) * C, :],
            preferred_element_type=F32,
        )
    return total


def conv_back(win_ref, field, weight_ref):
    total = jnp.zeros((ROWS, C), F32)
    for tap in range(27):
        total += lax.dot_general(
            tap_rows(win_ref, field, 26 - tap),
            weight_ref[tap * C : (tap + 1) * C, :],
            (((1,), (1,)), ((), ())),
            preferred_element_type=F32,
        )
    return total


def live_rows(counts_ref):
    return lax.broadcasted_iota(jnp.int32, (ROWS, C), 0) < counts_ref[0, 0] * 64


BLOCK = 216
TILES = 27
PACKED = 56


class Ring:
    def __init__(self, own, out, inbox, sends, recvs, me, right, left, place):
        self.own, self.out, self.inbox = own, out, inbox
        self.sends, self.recvs = sends, recvs
        self.me = place(me)
        self.to_right = place(lax.rem(me + 1, 4))
        self.to_left = place(lax.rem(me + 3, 4))
        across = place(lax.rem(me + 2, 4))
        self.half = own.shape[1] // 2
        self.plan = (
            (across, self.half, right),
            (across, 0, left),
            (self.to_right, 0, right),
            (self.to_left, self.half, left),
            (self.to_right, self.half, right),
            (self.to_left, 0, left),
        )

    def copy(self, index, piece):
        target, base, peer = self.plan[index]
        return pltpu.make_async_remote_copy(
            src_ref=self.out.at[target, base + piece],
            dst_ref=self.inbox.at[index, piece],
            send_sem=self.sends.at[index, piece],
            recv_sem=self.recvs.at[index, piece],
            device_id=peer,
            device_id_type=MESH,
        )

    def start(self, piece):
        for index in range(4):
            self.copy(index, piece).start()

    def relay(self, piece):
        for index in range(2):
            target, base, _ = self.plan[4 + index]
            self.copy(index, piece).wait_recv()
            total = self.own[target, base + piece] + self.inbox[index, piece].astype(F32)
            self.out[target, base + piece] = total.astype(BF16)
            self.copy(4 + index, piece).start()

    def arrive(self, piece):
        for index in range(2, 6):
            self.copy(index, piece).wait_recv()

    def total(self, piece, upper):
        first, second = (3, 4) if upper else (2, 5)
        mine = self.own[self.me, piece + self.half * upper]
        return mine + self.inbox[first, piece].astype(F32) + self.inbox[second, piece].astype(F32)

    def drain(self):
        for piece in range(self.half):
            for index in range(6):
                self.copy(index, piece).wait_send()


def ring_scratch(nz, rows):
    return [
        pltpu.VMEM((4, nz, rows, 128), F32),
        pltpu.VMEM((4, nz, rows, 128), BF16),
        pltpu.VMEM((6, nz // 2, rows, 128), BF16),
        pltpu.SemaphoreType.DMA((6, nz // 2)),
        pltpu.SemaphoreType.DMA((6, nz // 2)),
    ]


def reduce_scratch(nz):
    return (
        ring_scratch(nz, BLOCK) * 2
        + ring_scratch(nz, PACKED) * 2
        + [
            pltpu.VMEM((2, nz, PACKED, 128), F32),
            pltpu.VMEM((2, nz, PACKED, 128), F32),
            pltpu.VMEM((2, PACKED, 128), F32),
            pltpu.VMEM((PACKED, 128), F32),
            pltpu.SemaphoreType.DMA((2, nz)),
            pltpu.SemaphoreType.DMA((2, nz)),
            pltpu.SemaphoreType.DMA((2,)),
        ]
    )


def swapped(t):
    return lax.rem(t, 2) * 2 + t // 2


def straight(t):
    return t


def chip_place():
    gx, gy = lax.axis_index("gx"), lax.axis_index("gy")
    z, x, core, y = gx // 4, (lax.rem(gx, 4) // 2) * 2 + lax.rem(gy, 2), lax.rem(gx, 2), gy // 2
    return x, y, z, core


def device_at(x, y, z, core):
    return (z * 4 + (x // 2) * 2 + core, y * 2 + lax.rem(x, 2))


def reduce_peers(nz):
    x, y, z, core = chip_place()
    return (
        [device_at(x, y, z, 1 - core)]
        + [device_at(lax.rem(x + step, 4), y, z, core) for step in (1, 3)]
        + [device_at(x, lax.rem(y + step, 4), z, core) for step in (1, 3)]
        + [device_at(x, y, lax.rem(z + step, nz), core) for step in range(1, nz)]
    )


def spread(rows, own, out, z):
    lane = lax.broadcasted_iota(jnp.int32, (8, 128), 1) // 32
    tiles = rows.reshape(TILES, 8, 128)
    for target in range(4):
        packed = []
        for group in range(7):
            tile = None
            for part in range(4):
                index = 4 * group + part
                if index >= TILES:
                    continue
                shift = (part - target) % 4 * 32
                moved = pltpu.roll(tiles[index], shift, 1) if shift else tiles[index]
                tile = moved if tile is None else jnp.where(lane == part, moved, tile)
            packed.append(tile)
        block = jnp.concatenate(packed, axis=0)
        own[target, z] = block
        out[target, z] = block.astype(BF16)


def unspread(packed):
    tiles = packed.reshape(7, 8, 128)
    rows = []
    for index in range(TILES):
        part = index % 4
        tile = tiles[index // 4]
        rows.append(pltpu.roll(tile, 128 - 32 * part, 1) if part else tile)
    rows += [jnp.zeros((8, 128), F32)] * (32 - TILES)
    return jnp.concatenate(rows, axis=0).T[:32, :BLOCK]


class Reduce:
    def __init__(self, nz, scale, term, scratch):
        self.nz, self.scale, self.term, self.half = nz, scale, term, nz // 2
        self.clock = 0
        self.x, self.y, self.z, self.core = chip_place()
        x, y, z, core = self.x, self.y, self.z, self.core
        xs, ys, ys2, xs2 = (scratch[5 * i : 5 * i + 5] for i in range(4))
        self.zown, self.zin, self.last, self.got, self.zsend, self.zrecv, self.psem = scratch[20:]
        x_right = device_at(lax.rem(x + 1, 4), y, z, core)
        x_left = device_at(lax.rem(x + 3, 4), y, z, core)
        y_right = device_at(x, lax.rem(y + 1, 4), z, core)
        y_left = device_at(x, lax.rem(y + 3, 4), z, core)
        self.firsts = [
            Ring(*xs, x, x_right, x_left, straight),
            Ring(*ys, y, y_right, y_left, straight),
        ]
        self.seconds = [
            Ring(*ys2, y, y_right, y_left, swapped),
            Ring(*xs2, x, x_right, x_left, straight),
        ]

    def advance(self):
        for stage, step in enumerate((self.relay, self.turn, self.turn_relay, self.along)):
            piece = self.clock - 1 - stage
            if 0 <= piece < self.half:
                step(piece)
        self.clock += 1
        return self.clock <= self.half + 4

    def begin(self, piece):
        term = self.term
        lane = lax.broadcasted_iota(jnp.int32, (BLOCK, 128), 1)
        even = (lane // 32) % 2 == 0
        below = lane < 64

        def place(ring, target, z, value):
            ring.own[target, z] = value
            ring.out[target, z] = value.astype(BF16)

        ring = self.firsts[0]
        for z in (piece, piece + self.half):
            for half in range(2):
                start = (4 * z + 2 * half) * BLOCK
                left, right = (
                    term[start : start + BLOCK, :128],
                    term[start : start + BLOCK, 128:],
                )
                place(ring, 2 * half, z, jnp.where(even, left, pltpu.roll(right, 32, 1)))
                place(ring, 2 * half + 1, z, jnp.where(even, pltpu.roll(left, 96, 1), right))
        ring.start(piece)
        ring = self.firsts[1]
        for z in (piece, piece + self.half):
            for pair in range(2):
                zero, one = (
                    term[start : start + BLOCK, 128 * pair : 128 * pair + 128]
                    for start in ((4 * z + 1) * BLOCK, (4 * z + 3) * BLOCK)
                )
                place(ring, 2 * pair, z, jnp.where(below, zero, pltpu.roll(one, 64, 1)))
                place(ring, 2 * pair + 1, z, jnp.where(below, pltpu.roll(zero, 64, 1), one))
        ring.start(piece)

    def relay(self, piece):
        for ring in self.firsts:
            ring.relay(piece)

    def turn(self, piece):
        for ring, following in zip(self.firsts, self.seconds):
            ring.arrive(piece)
            for upper in range(2):
                spread(
                    ring.total(piece, upper),
                    following.own,
                    following.out,
                    piece + upper * self.half,
                )
            following.start(piece)

    def turn_relay(self, piece):
        for ring in self.seconds:
            ring.relay(piece)

    def zcopy(self, color, to_z, slot):
        return pltpu.make_async_remote_copy(
            src_ref=self.zown.at[color, to_z],
            dst_ref=self.zin.at[color, slot],
            send_sem=self.zsend.at[color, to_z],
            recv_sem=self.zrecv.at[color, slot],
            device_id=device_at(self.x, self.y, to_z, self.core),
            device_id_type=MESH,
        )

    def along(self, piece):
        for color, ring in enumerate(self.seconds):
            ring.arrive(piece)
            for upper in range(2):
                to_z = piece + upper * self.half
                self.zown[color, to_z] = ring.total(piece, upper)

                @pl.when(self.z != to_z)
                def _():
                    self.zcopy(color, to_z, self.z).start()

    def finish(self, first_ref, second_ref):
        for color in range(2):
            self.last[color] = self.zown[color, self.z]
            for from_z in range(self.nz):

                @pl.when(self.z != from_z)
                def _():
                    self.zcopy(color, from_z, from_z).wait_recv()
                    self.last[color] += self.zin[color, from_z]

        copy = pltpu.make_async_remote_copy(
            src_ref=self.last.at[1 - self.core],
            dst_ref=self.got,
            send_sem=self.psem.at[0],
            recv_sem=self.psem.at[1],
            device_id=device_at(self.x, self.y, self.z, 1 - self.core),
            device_id_type=MESH,
        )
        copy.start()
        for ring in self.firsts + self.seconds:
            ring.drain()
        for color in range(2):
            for to_z in range(self.nz):

                @pl.when(self.z != to_z)
                def _():
                    self.zcopy(color, to_z, self.z).wait_send()

        copy.wait()
        mine, other = self.last[self.core] * self.scale, self.got[...] * self.scale
        first = self.core == 0
        first_ref[...] = unspread(jnp.where(first, mine, other))
        second_ref[...] = unspread(jnp.where(first, other, mine))


def gradient_taps(piece, nz):
    needed = []
    for index in range(piece + 1):
        taps = set()
        for z in (index, index + nz // 2):
            taps |= set(range(864 * z // C, -(-864 * (z + 1) // C)))
        needed.append(taps)
    return sorted(needed[-1].difference(*needed[:-1]))


def runs(taps):
    out = []
    for tap in taps:
        if out and out[-1][1] == tap:
            out[-1][1] = tap + 1
        else:
            out.append([tap, tap + 1])
    return out


def step_kernel(
    nz,
    scale,
    feat_hbm,
    cot_hbm,
    pick_hbm,
    table_hbm,
    coords_ref,
    counts_ref,
    w1_hbm,
    w2_hbm,
    out_hbm,
    grad_hbm,
    first_hbm,
    second_hbm,
    out_ref,
    grad_ref,
    first_ref,
    second_ref,
    put_sems,
    feat,
    cot,
    pick,
    table,
    w1,
    w2,
    load_sems,
    packed,
    landed,
    send_sems,
    recv_sems,
    sent_code,
    codes_in,
    code_send,
    code_recv,
    code,
    win,
    rows,
    pair_win,
    pair_rows,
    pair_sems,
    turned,
    term,
    *scratch,
):
    nx, ny = lax.axis_size("gx"), lax.axis_size("gy")
    gx, gy = lax.axis_index("gx"), lax.axis_index("gy")
    x, y, z, core = chip_place()
    peers = around() + reduce_peers(nz)
    barrier = pltpu.get_barrier_semaphore()
    for peer in peers:
        pl.semaphore_signal(barrier, inc=1, device_id=peer, device_id_type=MESH)
    loads = [
        pltpu.make_async_copy(source, target, load_sems.at[index])
        for index, (source, target) in enumerate(
            (
                (feat_hbm, feat),
                (cot_hbm, cot),
                (pick_hbm, pick),
                (table_hbm, table),
                (w1_hbm, w1),
                (w2_hbm, w2),
            )
        )
    ]
    for load in loads:
        load.start()
    for load in loads[:4]:
        load.wait()
    blocks = block_codes(coords_ref, counts_ref)
    to_x = gx + table[2:3, :]
    to_y = gy + table[3:4, :]
    inside = (to_x >= 0) & (to_x < nx) & (to_y >= 0) & (to_y < ny)
    sent = table[1:2, :] + by_slot(table[0:1, :], blocks)
    sent_code[...] = jnp.broadcast_to(jnp.where(inside, sent, DEAD), (8, FACE))
    packed[0, 0] = jnp.dot(pick[...], feat[...], preferred_element_type=F32).astype(BF16)
    packed[0, 1] = jnp.dot(pick[...], cot[...], preferred_element_type=F32).astype(BF16)
    pl.semaphore_wait(barrier, len(peers))
    faces = swap_faces(
        packed.at[0],
        landed.at[0],
        send_sems.at[0],
        recv_sems.at[0],
        ((sent_code, codes_in, code_send, code_recv),),
    )
    for copy in faces:
        copy.start()
    lane = lax.broadcasted_iota(jnp.int32, (8, ROWS), 1)
    voxel = lane % 64
    own = (voxel // 16 + 1) * 4096 + ((voxel // 4) % 4 + 1) * 64 + voxel % 4 + 1
    code[:, FACE:] = own + by_slot(lane // 64, blocks)
    live = live_rows(counts_ref)
    region = jnp.broadcast_to(table[4:5, :], (8, FACE))
    for copy in faces:
        copy.wait_recv()
    got = codes_in[0]
    for index in range(1, 8):
        got = jnp.where(region == index, codes_in[index], got)
    code[:, :FACE] = got
    build_windows(
        jnp.concatenate([landed[0, 0], feat[...]], axis=0),
        jnp.concatenate([landed[0, 1], cot[...]], axis=0),
        code,
        coords_ref,
        win.at[0],
    )
    pair = [
        pltpu.make_async_remote_copy(
            src_ref=source,
            dst_ref=target,
            send_sem=pair_sems.at[2 * index],
            recv_sem=pair_sems.at[2 * index + 1],
            device_id=device_at(x, y, z, 1 - core),
            device_id_type=MESH,
        )
        for index, (source, target) in enumerate(
            ((win.at[0, 1 - core], pair_win), (rows.at[core], pair_rows))
        )
    ]
    pair[0].start()
    loads[4].wait()
    pre = conv(win.at[0], 0, w1)
    gate = jax.nn.sigmoid(pre)
    hidden = jnp.where(live, pre * gate, 0.0).astype(BF16)
    rows[0] = hidden
    packed[1, 0] = jnp.dot(pick[...], hidden, preferred_element_type=F32).astype(BF16)
    loads[5].wait()
    hidden_grad = conv_back(win.at[0], 1, w2)
    pre_grad = jnp.where(live, hidden_grad * gate * (1.0 + pre * (1.0 - gate)), 0.0).astype(BF16)
    rows[1] = pre_grad
    packed[1, 1] = jnp.dot(pick[...], pre_grad, preferred_element_type=F32).astype(BF16)
    pair[1].start()
    more_faces = swap_faces(
        packed.at[1], landed.at[1], send_sems.at[1], recv_sems.at[1]
    )
    for copy in more_faces:
        copy.start()
    for copy in pair:
        copy.wait_recv()

    def window(tap):
        shift, start = lax.rem(tap, 9), tap // 9
        return jnp.concatenate(
            [
                win[0, core, shift, :, pl.ds(start, 4)].reshape(ROWS, C),
                pair_win[shift, :, pl.ds(start, 4)].reshape(ROWS, C),
            ],
            axis=0,
        )

    both = jnp.concatenate([rows[1 - core], pair_rows[...]], axis=0)
    turned[...] = both.astype(F32).T.astype(BF16)
    reduce = Reduce(nz, scale, term, scratch)
    for piece in range(nz // 2):
        for start, stop in runs(gradient_taps(piece, nz)):

            @pl.when(core == 0)
            def _():
                @pl.loop(start, stop)
                def _(tap):
                    term[pl.ds(pl.multiple_of(tap * C, C), C), :] = lax.dot_general(
                        window(tap),
                        jnp.concatenate([rows[1], pair_rows[...]], axis=0),
                        (((0,), (0,)), ((), ())),
                        preferred_element_type=F32,
                    )

            @pl.when(core == 1)
            def _():
                @pl.loop(start, stop)
                def _(tap):
                    term[pl.ds(pl.multiple_of(tap * C, C), C), :] = jnp.dot(
                        turned[...], window(26 - tap), preferred_element_type=F32
                    )

        reduce.begin(piece)
        reduce.advance()
    for copy in more_faces:
        copy.wait_recv()
    build_windows(
        jnp.concatenate([landed[1, 0], rows[0]], axis=0),
        jnp.concatenate([landed[1, 1], rows[1]], axis=0),
        code,
        coords_ref,
        win.at[1],
    )
    reduce.advance()
    out_ref[...] = jnp.where(live, conv(win.at[1], 0, w2), 0.0)
    puts = [
        pltpu.make_async_copy(source, target, put_sems.at[index])
        for index, (source, target) in enumerate(
            (
                (out_ref, out_hbm),
                (grad_ref, grad_hbm),
                (first_ref, first_hbm),
                (second_ref, second_hbm),
            )
        )
    ]
    puts[0].start()
    reduce.advance()
    grad_ref[...] = jnp.where(live, conv_back(win.at[1], 1, w1), 0.0)
    puts[1].start()
    while reduce.advance():
        pass
    for copy in faces + more_faces + pair:
        copy.wait_send()
    reduce.finish(first_ref, second_ref)
    for put in puts[2:]:
        put.start()
    for put in puts:
        put.wait()


def store_kernel(*refs):
    sources, targets, held, sems = refs[:4], refs[4:8], refs[8:12], refs[12]
    takes = [
        pltpu.make_async_copy(sources[index], held[index], sems.at[index]) for index in range(4)
    ]
    puts = [
        pltpu.make_async_copy(held[index], targets[index], sems.at[4 + index])
        for index in range(4)
    ]
    for take in takes:
        take.start()
    for take, put in zip(takes, puts):
        take.wait()
        put.start()
    for put in puts:
        put.wait()


def vmem():
    return pl.BlockSpec(memory_space=pltpu.VMEM)


def smem():
    return pl.BlockSpec(memory_space=pltpu.SMEM)


def hbm():
    return pl.BlockSpec(memory_space=pltpu.HBM)


def per_device(features, block_coords, block_counts, first_weight, second_weight, cotangent):
    feat = features.reshape(ROWS, C)
    cot = cotangent.reshape(ROWS, C)
    coords = block_coords.reshape(1, SLOTS)
    counts = block_counts.reshape(1, 1)
    pick_np, table_np = face_tables()
    pick = jnp.asarray(pick_np, BF16)
    table = jnp.asarray(table_np)
    struct = jax.ShapeDtypeStruct
    scale = 1.0 / math.sqrt(64 * SLOTS * lax.axis_size("gx") * lax.axis_size("gy"))
    nz = lax.axis_size("gx") // 4
    window = (9, SLOTS, 6, 16, C)
    dma = pltpu.SemaphoreType.DMA
    out, grad, first_grad, second_grad = pl.pallas_call(
        functools.partial(step_kernel, nz, scale),
        out_shape=(
            struct((ROWS, C), F32),
            struct((ROWS, C), F32),
            struct((32, BLOCK), F32),
            struct((32, BLOCK), F32),
        ),
        in_specs=[hbm()] * 4 + [smem()] * 2 + [hbm()] * 2,
        out_specs=(hbm(),) * 4,
        scratch_shapes=[
            pltpu.VMEM((ROWS, C), F32),
            pltpu.VMEM((ROWS, C), F32),
            pltpu.VMEM((32, BLOCK), F32),
            pltpu.VMEM((32, BLOCK), F32),
            dma((4,)),
            pltpu.VMEM((ROWS, C), BF16),
            pltpu.VMEM((ROWS, C), BF16),
            pltpu.VMEM((FACE, ROWS), BF16),
            pltpu.VMEM((8, FACE), jnp.int32),
            pltpu.VMEM((27 * C, C), BF16),
            pltpu.VMEM((27 * C, C), BF16),
            dma((6,)),
            pltpu.VMEM((2, 2, FACE, C), BF16),
            pltpu.VMEM((2, 2, FACE, C), BF16),
            dma((2, 8)),
            dma((2, 8)),
            pltpu.VMEM((8, FACE), jnp.int32),
            pltpu.VMEM((8, 8, FACE), jnp.int32),
            dma((8,)),
            dma((8,)),
            pltpu.VMEM((8, DATA), jnp.int32),
            pltpu.VMEM((2, 2) + window, BF16),
            pltpu.VMEM((2, ROWS, C), BF16),
            pltpu.VMEM(window, BF16),
            pltpu.VMEM((ROWS, C), BF16),
            dma((4,)),
            pltpu.VMEM((C, 2 * ROWS), BF16),
            pltpu.VMEM((27 * C, C), F32),
        ]
        + reduce_scratch(nz),
        compiler_params=pltpu.CompilerParams(
            collective_id=0, has_side_effects=True, vmem_limit_bytes=LIMIT
        ),
        name="step",
    )(feat, cot, pick, table, coords, counts, first_weight, second_weight)
    results = (out, grad, first_grad, second_grad)
    out, grad, first_grad, second_grad = pl.pallas_call(
        store_kernel,
        out_shape=[struct(result.shape, F32) for result in results],
        in_specs=[hbm()] * 4,
        out_specs=[hbm()] * 4,
        scratch_shapes=[pltpu.VMEM(result.shape, F32) for result in results] + [dma((8,))],
        name="store",
    )(*results)
    return out.reshape(features.shape), grad.reshape(features.shape), first_grad.T, second_grad.T


def solution(mesh):
    placed = (
        P("gx", "gy", None, None, None),
        P("gx", "gy", None),
        P("gx", "gy"),
        P(),
        P(),
        P("gx", "gy", None, None, None),
    )
    return jax.shard_map(
        per_device,
        mesh=mesh,
        in_specs=placed,
        out_specs=(
            P("gx", "gy", None, None, None),
            P("gx", "gy", None, None, None),
            P("gx", "gy"),
            P("gx", "gy"),
        ),
        check_vma=False,
    )
```

```python
import functools
import math

import jax
import jax.numpy as jnp
import numpy as np
from jax import lax
from jax.experimental import pallas as pl
from jax.experimental.pallas import tpu as pltpu
from jax.sharding import PartitionSpec as P

C = 256
SLOTS = 3
ROWS = 192
FACE = 256
DATA = FACE + ROWS
DEAD = -(1 << 24)
LIMIT = 58 << 20
MESH = pl.DeviceIdType.MESH
F32 = jnp.float32
BF16 = jnp.bfloat16

REGIONS = (
    (-1, 0, 0, 48),
    (1, 0, 48, 48),
    (0, -1, 96, 48),
    (0, 1, 144, 48),
    (-1, -1, 192, 16),
    (-1, 1, 208, 16),
    (1, -1, 224, 16),
    (1, 1, 240, 16),
)


def face_tables():
    source = np.full(FACE, -1, np.int64)
    table = np.zeros((8, FACE), np.int32)
    table[1] = DEAD
    for sx, sy, start, _ in REGIONS:
        xs = range(4) if sx == 0 else ((3,) if sx < 0 else (0,))
        ys = range(4) if sy == 0 else ((3,) if sy < 0 else (0,))
        row = start
        for slot in range(SLOTS):
            for vx in xs:
                for vy in ys:
                    for vz in range(4):
                        source[row] = slot * 64 + vx * 16 + vy * 4 + vz
                        table[0, row] = slot
                        table[1, row] = (
                            (8 * sx + vx + 1) * 4096 + (8 * sy + vy + 1) * 64 + vz + 1
                        )
                        row += 1
        table[2, start : start + (48 if sx * sy == 0 else 16)] = -sx
        table[3, start : start + (48 if sx * sy == 0 else 16)] = -sy
    for index, (_, _, start, count) in enumerate(REGIONS):
        table[4, start : start + count] = index
    pick = (source[:, None] == np.arange(ROWS)[None, :]).astype(np.float32)
    return pick, table


def block_codes(coords_ref, counts_ref):
    codes = []
    for slot in range(SLOTS):
        p = coords_ref[0, slot]
        code = (p // 16) * (4 * 4096) + ((p // 8) % 2) * (4 * 64) + (p % 8) * 4
        codes.append((code, slot < counts_ref[0, 0]))
    return codes


def by_slot(slot, codes):
    values = [jnp.where(live, code, DEAD) for code, live in codes]
    return jnp.where(slot == 0, values[0], jnp.where(slot == 1, values[1], values[2]))


def swap_faces(packed, landed, send_sems, recv_sems, index_last=False):
    copies = []
    for index, (peer, (_, _, start, count)) in enumerate(zip(around(), REGIONS)):
        part = pl.ds(start, count)
        copies.append(
            pltpu.make_async_remote_copy(
                src_ref=packed if index_last else packed.at[part],
                dst_ref=landed.at[index] if index_last else landed.at[part],
                send_sem=send_sems.at[index],
                recv_sem=recv_sems.at[index],
                device_id=peer,
                device_id_type=MESH,
            )
        )
    return copies


def around():
    nx, ny = lax.axis_size("gx"), lax.axis_size("gy")
    gx, gy = lax.axis_index("gx"), lax.axis_index("gy")
    return [
        (lax.rem(gx - sx + nx, nx), lax.rem(gy - sy + ny, ny)) for sx, sy, _, _ in REGIONS
    ]


def build_placing(code, coords_ref, placing):
    row = lax.broadcasted_iota(jnp.int32, (96, DATA), 0)
    pattern = (row // 16) * 4096 + ((row // 4) % 4) * 64 + row % 4
    offset = jnp.broadcast_to(code, (96, DATA)) - pattern
    for slot in range(SLOTS):
        p = coords_ref[0, slot]
        start = (p // 16) * (4 * 4096) + ((p // 8) % 2) * (4 * 64) + (p % 8) * 4
        for shift in range(9):
            placing[shift, slot * 96 : slot * 96 + 96, :] = jnp.where(
                offset == start + (shift // 3) * 64 + shift % 3, 1.0, 0.0
            ).astype(BF16)


def build_windows(landed, own, placing, win_ref):
    data = jnp.concatenate([landed, own], axis=0)
    for shift in range(9):
        rows = jnp.dot(placing[shift], data, preferred_element_type=F32).astype(BF16)
        win_ref[shift] = rows.reshape(SLOTS, 6, 16, C)


def tap_rows(win_ref, tap):
    return win_ref[tap % 9, :, tap // 9 : tap // 9 + 4].reshape(ROWS, C)


def conv(win_ref, weight_ref):
    total = jnp.zeros((ROWS, C), F32)
    for tap in range(27):
        total += jnp.dot(
            tap_rows(win_ref, tap),
            weight_ref[tap * C : (tap + 1) * C, :],
            preferred_element_type=F32,
        )
    return total


def conv_back(win_ref, weight_ref):
    total = jnp.zeros((ROWS, C), F32)
    for tap in range(27):
        total += lax.dot_general(
            tap_rows(win_ref, 26 - tap),
            weight_ref[tap * C : (tap + 1) * C, :],
            (((1,), (1,)), ((), ())),
            preferred_element_type=F32,
        )
    return total


def live_rows(counts_ref):
    return lax.broadcasted_iota(jnp.int32, (ROWS, C), 0) < counts_ref[0, 0] * 64


BLOCK = 216
TILES = 27
PACKED = 56


class Ring:
    def __init__(self, own, out, inbox, sends, recvs, me, right, left, place):
        self.own, self.out, self.inbox = own, out, inbox
        self.sends, self.recvs = sends, recvs
        self.me = place(me)
        self.to_right = place(lax.rem(me + 1, 4))
        self.to_left = place(lax.rem(me + 3, 4))
        across = place(lax.rem(me + 2, 4))
        self.half = own.shape[1] // 2
        self.plan = (
            (across, self.half, right),
            (across, 0, left),
            (self.to_right, 0, right),
            (self.to_left, self.half, left),
            (self.to_right, self.half, right),
            (self.to_left, 0, left),
        )

    def copy(self, index, piece):
        target, base, peer = self.plan[index]
        return pltpu.make_async_remote_copy(
            src_ref=self.out.at[target, base + piece],
            dst_ref=self.inbox.at[index, piece],
            send_sem=self.sends.at[index, piece],
            recv_sem=self.recvs.at[index, piece],
            device_id=peer,
            device_id_type=MESH,
        )

    def start(self, piece):
        for index in range(4):
            self.copy(index, piece).start()

    def relay(self, piece):
        for index in range(2):
            target, base, _ = self.plan[4 + index]
            self.copy(index, piece).wait_recv()
            total = self.own[target, base + piece] + self.inbox[index, piece].astype(F32)
            self.out[target, base + piece] = total.astype(BF16)
            self.copy(4 + index, piece).start()

    def arrive(self, piece):
        for index in range(2, 6):
            self.copy(index, piece).wait_recv()

    def total(self, piece, upper):
        first, second = (3, 4) if upper else (2, 5)
        mine = self.own[self.me, piece + self.half * upper]
        return mine + self.inbox[first, piece].astype(F32) + self.inbox[second, piece].astype(F32)

    def drain(self):
        for piece in range(self.half):
            for index in range(6):
                self.copy(index, piece).wait_send()


def ring_scratch(nz, rows):
    return [
        pltpu.VMEM((4, nz, rows, 128), F32),
        pltpu.VMEM((4, nz, rows, 128), BF16),
        pltpu.VMEM((6, nz // 2, rows, 128), BF16),
        pltpu.SemaphoreType.DMA((6, nz // 2)),
        pltpu.SemaphoreType.DMA((6, nz // 2)),
    ]


def reduce_scratch(nz):
    return (
        ring_scratch(nz, BLOCK) * 2
        + ring_scratch(nz, PACKED) * 2
        + [
            pltpu.VMEM((2, nz, PACKED, 128), F32),
            pltpu.VMEM((2, nz, PACKED, 128), F32),
            pltpu.VMEM((2, nz, PACKED, 128), BF16),
            pltpu.VMEM((2, nz, PACKED, 128), BF16),
            pltpu.VMEM((2, PACKED, 128), F32),
            pltpu.SemaphoreType.DMA((2, nz)),
            pltpu.SemaphoreType.DMA((2, nz)),
        ]
    )


def swapped(t):
    return lax.rem(t, 2) * 2 + t // 2


def straight(t):
    return t


def chip_place():
    gx, gy = lax.axis_index("gx"), lax.axis_index("gy")
    z, x, core, y = gx // 4, (lax.rem(gx, 4) // 2) * 2 + lax.rem(gy, 2), lax.rem(gx, 2), gy // 2
    return x, y, z, core


def device_at(x, y, z, core):
    return (z * 4 + (x // 2) * 2 + core, y * 2 + lax.rem(x, 2))


def reduce_peers(nz):
    x, y, z, core = chip_place()
    return (
        [device_at(x, y, z, 1 - core)]
        + [device_at(lax.rem(x + step, 4), y, z, core) for step in (1, 3)]
        + [device_at(x, lax.rem(y + step, 4), z, core) for step in (1, 3)]
        + [device_at(x, y, lax.rem(z + step, nz), c) for step in range(1, nz) for c in range(2)]
    )


def spread(rows, own, out, z):
    lane = lax.broadcasted_iota(jnp.int32, (8, 128), 1) // 32
    tiles = rows.reshape(TILES, 8, 128)
    for target in range(4):
        packed = []
        for group in range(7):
            tile = None
            for part in range(4):
                index = 4 * group + part
                if index >= TILES:
                    continue
                shift = (part - target) % 4 * 32
                moved = pltpu.roll(tiles[index], shift, 1) if shift else tiles[index]
                tile = moved if tile is None else jnp.where(lane == part, moved, tile)
            packed.append(tile)
        block = jnp.concatenate(packed, axis=0)
        own[target, z] = block
        out[target, z] = block.astype(BF16)


def unspread(packed):
    tiles = packed.reshape(7, 8, 128)
    rows = []
    for index in range(TILES):
        part = index % 4
        tile = tiles[index // 4]
        rows.append(pltpu.roll(tile, 128 - 32 * part, 1) if part else tile)
    rows += [jnp.zeros((8, 128), F32)] * (32 - TILES)
    return jnp.concatenate(rows, axis=0).T[:32, :BLOCK]


class Reduce:
    def __init__(self, nz, scale, term, scratch):
        self.nz, self.scale, self.term, self.half = nz, scale, term, nz // 2
        self.clock = 0
        self.x, self.y, self.z, self.core = chip_place()
        x, y, z, core = self.x, self.y, self.z, self.core
        xs, ys, ys2, xs2 = (scratch[5 * i : 5 * i + 5] for i in range(4))
        self.zown, self.zin, self.zout, self.zlate, self.last, self.zsend, self.zrecv = scratch[20:]
        x_right = device_at(lax.rem(x + 1, 4), y, z, core)
        x_left = device_at(lax.rem(x + 3, 4), y, z, core)
        y_right = device_at(x, lax.rem(y + 1, 4), z, core)
        y_left = device_at(x, lax.rem(y + 3, 4), z, core)
        self.firsts = [
            Ring(*xs, x, x_right, x_left, straight),
            Ring(*ys, y, y_right, y_left, straight),
        ]
        self.seconds = [
            Ring(*ys2, y, y_right, y_left, swapped),
            Ring(*xs2, x, x_right, x_left, straight),
        ]

    def advance(self):
        for stage, step in enumerate((self.relay, self.turn, self.turn_relay, self.along)):
            piece = self.clock - 1 - stage
            if 0 <= piece < self.half:
                step(piece)
        self.clock += 1
        return self.clock <= self.half + 4

    def begin(self, piece):
        term = self.term
        lane = lax.broadcasted_iota(jnp.int32, (BLOCK, 128), 1)
        even = (lane // 32) % 2 == 0
        below = lane < 64

        def place(ring, target, z, value):
            ring.own[target, z] = value
            ring.out[target, z] = value.astype(BF16)

        ring = self.firsts[0]
        for z in (piece, piece + self.half):
            for half in range(2):
                start = (4 * z + 2 * half) * BLOCK
                left, right = (
                    term[start : start + BLOCK, :128],
                    term[start : start + BLOCK, 128:],
                )
                place(ring, 2 * half, z, jnp.where(even, left, pltpu.roll(right, 32, 1)))
                place(ring, 2 * half + 1, z, jnp.where(even, pltpu.roll(left, 96, 1), right))
        ring.start(piece)
        ring = self.firsts[1]
        for z in (piece, piece + self.half):
            for pair in range(2):
                zero, one = (
                    term[start : start + BLOCK, 128 * pair : 128 * pair + 128]
                    for start in ((4 * z + 1) * BLOCK, (4 * z + 3) * BLOCK)
                )
                place(ring, 2 * pair, z, jnp.where(below, zero, pltpu.roll(one, 64, 1)))
                place(ring, 2 * pair + 1, z, jnp.where(below, pltpu.roll(zero, 64, 1), one))
        ring.start(piece)

    def relay(self, piece):
        for ring in self.firsts:
            ring.relay(piece)

    def turn(self, piece):
        for ring, following in zip(self.firsts, self.seconds):
            ring.arrive(piece)
            for upper in range(2):
                spread(
                    ring.total(piece, upper),
                    following.own,
                    following.out,
                    piece + upper * self.half,
                )
            following.start(piece)

    def turn_relay(self, piece):
        for ring in self.seconds:
            ring.relay(piece)

    def zcopy(self, color, to_z, source, slot):
        late = to_z % self.half == self.half - 1
        return pltpu.make_async_remote_copy(
            src_ref=(self.zout if late else self.zown).at[color, to_z],
            dst_ref=(self.zlate if late else self.zin).at[source, slot],
            send_sem=self.zsend.at[color, to_z],
            recv_sem=self.zrecv.at[source, slot],
            device_id=device_at(self.x, self.y, to_z, color),
            device_id_type=MESH,
        )

    def along(self, piece):
        for color, ring in enumerate(self.seconds):
            ring.arrive(piece)
            for upper in range(2):
                to_z = piece + upper * self.half
                total = ring.total(piece, upper)
                self.zown[color, to_z] = total
                if piece == self.half - 1:
                    self.zout[color, to_z] = total.astype(BF16)

                @pl.when((self.z != to_z) | (self.core != color))
                def _():
                    self.zcopy(color, to_z, self.core, self.z).start()

    def gather(self, late):
        inbox, to_z = (self.zlate, self.half - 1) if late else (self.zin, 0)
        for source in range(2):
            for from_z in range(self.nz):

                @pl.when((self.z != from_z) | (self.core != source))
                def _():
                    self.zcopy(0, to_z, source, from_z).wait_recv()
                    self.last[source] += inbox[source, from_z].astype(F32)

    def finish(self, first_ref, second_ref):
        self.last[self.core] = self.zown[self.core, self.z]
        self.last[1 - self.core] = jnp.zeros((PACKED, 128), F32)
        late = lax.rem(self.z, self.half) == self.half - 1

        @pl.when(late)
        def _():
            self.gather(True)

        @pl.when(jnp.logical_not(late))
        def _():
            self.gather(False)

        first_ref[...] = unspread(self.last[0] * self.scale)
        second_ref[...] = unspread(self.last[1] * self.scale)

    def drain(self):
        for ring in self.firsts + self.seconds:
            ring.drain()
        for color in range(2):
            for to_z in range(self.nz):

                @pl.when((self.z != to_z) | (self.core != color))
                def _():
                    self.zcopy(color, to_z, self.core, self.z).wait_send()


def gradient_taps(piece, nz):
    needed = []
    for index in range(piece + 1):
        taps = set()
        for z in (index, index + nz // 2):
            taps |= set(range(864 * z // C, -(-864 * (z + 1) // C)))
        needed.append(taps)
    return sorted(needed[-1].difference(*needed[:-1]))


def runs(taps):
    out = []
    for tap in taps:
        if out and out[-1][1] == tap:
            out[-1][1] = tap + 1
        else:
            out.append([tap, tap + 1])
    return out


def step_kernel(
    nz,
    scale,
    feat_hbm,
    cot_hbm,
    pick_hbm,
    table_hbm,
    coords_ref,
    counts_ref,
    w1_hbm,
    w2_hbm,
    out_hbm,
    grad_hbm,
    first_hbm,
    second_hbm,
    out_ref,
    grad_ref,
    first_ref,
    second_ref,
    put_sems,
    feat,
    cot,
    pick,
    table,
    w1,
    w2,
    load_sems,
    packed,
    landed,
    send_sems,
    recv_sems,
    sent_code,
    codes_in,
    code_send,
    code_recv,
    placing,
    win,
    rows,
    pair_win,
    pair_rows,
    pair_sems,
    turned,
    term,
    *scratch,
):
    nx, ny = lax.axis_size("gx"), lax.axis_size("gy")
    gx, gy = lax.axis_index("gx"), lax.axis_index("gy")
    x, y, z, core = chip_place()
    peers = around() + reduce_peers(nz)
    barrier = pltpu.get_barrier_semaphore()
    for peer in peers:
        pl.semaphore_signal(barrier, inc=1, device_id=peer, device_id_type=MESH)
    loads = [
        pltpu.make_async_copy(source, target, load_sems.at[index])
        for index, (source, target) in enumerate(
            (
                (feat_hbm, feat),
                (cot_hbm, cot),
                (pick_hbm, pick),
                (table_hbm, table),
                (w1_hbm, w1),
                (w2_hbm, w2),
            )
        )
    ]
    for load in loads:
        load.start()
    for load in loads[:4]:
        load.wait()
    blocks = block_codes(coords_ref, counts_ref)
    to_x = gx + table[2:3, :]
    to_y = gy + table[3:4, :]
    inside = (to_x >= 0) & (to_x < nx) & (to_y >= 0) & (to_y < ny)
    sent = table[1:2, :] + by_slot(table[0:1, :], blocks)
    sent_code[...] = jnp.broadcast_to(jnp.where(inside, sent, DEAD), (8, FACE))
    packed[0, 0] = jnp.dot(pick[...], feat[...], preferred_element_type=F32).astype(BF16)
    packed[0, 1] = jnp.dot(pick[...], cot[...], preferred_element_type=F32).astype(BF16)
    faces = [
        swap_faces(
            packed.at[phase, field],
            landed.at[phase, field],
            send_sems.at[phase, field],
            recv_sems.at[phase, field],
        )
        for phase in range(2)
        for field in range(2)
    ]
    code_copies = swap_faces(sent_code, codes_in, code_send, code_recv, True)
    pl.semaphore_wait(barrier, len(peers))
    for copy in code_copies + faces[0] + faces[1]:
        copy.start()
    lane = lax.broadcasted_iota(jnp.int32, (8, ROWS), 1)
    voxel = lane % 64
    own = (voxel // 16 + 1) * 4096 + ((voxel // 4) % 4 + 1) * 64 + voxel % 4 + 1
    own += by_slot(lane // 64, blocks)
    live = live_rows(counts_ref)
    region = jnp.broadcast_to(table[4:5, :], (8, FACE))
    for copy in code_copies:
        copy.wait_recv()
    got = codes_in[0]
    for index in range(1, 8):
        got = jnp.where(region == index, codes_in[index], got)
    code = jnp.concatenate([got, own], axis=1)[0:1, :]
    build_placing(code, coords_ref, placing)
    for copy in faces[0]:
        copy.wait_recv()
    build_windows(landed[0, 0], feat[...], placing, win.at[0, 0])
    pair = [
        pltpu.make_async_remote_copy(
            src_ref=source,
            dst_ref=target,
            send_sem=pair_sems.at[2 * index],
            recv_sem=pair_sems.at[2 * index + 1],
            device_id=device_at(x, y, z, 1 - core),
            device_id_type=MESH,
        )
        for index, (source, target) in enumerate(
            ((win.at[0, 1 - core], pair_win), (rows.at[core], pair_rows))
        )
    ]
    loads[4].wait()
    pre = conv(win.at[0, 0], w1)
    gate = jax.nn.sigmoid(pre)
    hidden = jnp.where(live, pre * gate, 0.0).astype(BF16)
    rows[0] = hidden
    packed[1, 0] = jnp.dot(pick[...], hidden, preferred_element_type=F32).astype(BF16)
    for copy in faces[1]:
        copy.wait_recv()
    build_windows(landed[0, 1], cot[...], placing, win.at[0, 1])
    pair[0].start()
    loads[5].wait()
    hidden_grad = conv_back(win.at[0, 1], w2)
    pre_grad = jnp.where(live, hidden_grad * gate * (1.0 + pre * (1.0 - gate)), 0.0).astype(BF16)
    rows[1] = pre_grad
    packed[1, 1] = jnp.dot(pick[...], pre_grad, preferred_element_type=F32).astype(BF16)
    pair[1].start()
    for copy in faces[2] + faces[3]:
        copy.start()
    for copy in pair:
        copy.wait_recv()

    def window(tap):
        shift, start = lax.rem(tap, 9), tap // 9
        return jnp.concatenate(
            [
                win[0, core, shift, :, pl.ds(start, 4)].reshape(ROWS, C),
                pair_win[shift, :, pl.ds(start, 4)].reshape(ROWS, C),
            ],
            axis=0,
        )

    both = jnp.concatenate([rows[1 - core], pair_rows[...]], axis=0)
    turned[...] = both.astype(F32).T.astype(BF16)
    reduce = Reduce(nz, scale, term, scratch)
    for piece in range(nz // 2):
        for start, stop in runs(gradient_taps(piece, nz)):

            @pl.when(core == 0)
            def _():
                @pl.loop(start, stop)
                def _(tap):
                    term[pl.ds(pl.multiple_of(tap * C, C), C), :] = lax.dot_general(
                        window(tap),
                        jnp.concatenate([rows[1], pair_rows[...]], axis=0),
                        (((0,), (0,)), ((), ())),
                        preferred_element_type=F32,
                    )

            @pl.when(core == 1)
            def _():
                @pl.loop(start, stop)
                def _(tap):
                    term[pl.ds(pl.multiple_of(tap * C, C), C), :] = jnp.dot(
                        turned[...], window(26 - tap), preferred_element_type=F32
                    )

        reduce.begin(piece)
        reduce.advance()
    for field in range(2):
        for copy in faces[2 + field]:
            copy.wait_recv()
        build_windows(landed[1, field], rows[field], placing, win.at[1, field])
    reduce.advance()
    out_ref[...] = jnp.where(live, conv(win.at[1, 0], w2), 0.0)
    puts = [
        pltpu.make_async_copy(source, target, put_sems.at[index])
        for index, (source, target) in enumerate(
            (
                (out_ref, out_hbm),
                (grad_ref, grad_hbm),
                (first_ref, first_hbm),
                (second_ref, second_hbm),
            )
        )
    ]
    puts[0].start()
    reduce.advance()
    grad_ref[...] = jnp.where(live, conv_back(win.at[1, 1], w1), 0.0)
    puts[1].start()
    while reduce.advance():
        pass
    reduce.finish(first_ref, second_ref)
    for put in puts[2:]:
        put.start()
    for copy in code_copies + sum(faces, []) + pair:
        copy.wait_send()
    reduce.drain()
    for put in puts:
        put.wait()


def store_kernel(*refs):
    sources, targets, held, sems = refs[:4], refs[4:8], refs[8:12], refs[12]
    takes = [
        pltpu.make_async_copy(sources[index], held[index], sems.at[index]) for index in range(4)
    ]
    puts = [
        pltpu.make_async_copy(held[index], targets[index], sems.at[4 + index])
        for index in range(4)
    ]
    for take in takes:
        take.start()
    for take, put in zip(takes, puts):
        take.wait()
        put.start()
    for put in puts:
        put.wait()


def vmem():
    return pl.BlockSpec(memory_space=pltpu.VMEM)


def smem():
    return pl.BlockSpec(memory_space=pltpu.SMEM)


def hbm():
    return pl.BlockSpec(memory_space=pltpu.HBM)


def per_device(features, block_coords, block_counts, first_weight, second_weight, cotangent):
    feat = features.reshape(ROWS, C)
    cot = cotangent.reshape(ROWS, C)
    coords = block_coords.reshape(1, SLOTS)
    counts = block_counts.reshape(1, 1)
    pick_np, table_np = face_tables()
    pick = jnp.asarray(pick_np, BF16)
    table = jnp.asarray(table_np)
    struct = jax.ShapeDtypeStruct
    scale = 1.0 / math.sqrt(64 * SLOTS * lax.axis_size("gx") * lax.axis_size("gy"))
    nz = lax.axis_size("gx") // 4
    window = (9, SLOTS, 6, 16, C)
    dma = pltpu.SemaphoreType.DMA
    out, grad, first_grad, second_grad = pl.pallas_call(
        functools.partial(step_kernel, nz, scale),
        out_shape=(
            struct((ROWS, C), F32),
            struct((ROWS, C), F32),
            struct((32, BLOCK), F32),
            struct((32, BLOCK), F32),
        ),
        in_specs=[hbm()] * 4 + [smem()] * 2 + [hbm()] * 2,
        out_specs=(hbm(),) * 4,
        scratch_shapes=[
            pltpu.VMEM((ROWS, C), F32),
            pltpu.VMEM((ROWS, C), F32),
            pltpu.VMEM((32, BLOCK), F32),
            pltpu.VMEM((32, BLOCK), F32),
            dma((4,)),
            pltpu.VMEM((ROWS, C), BF16),
            pltpu.VMEM((ROWS, C), BF16),
            pltpu.VMEM((FACE, ROWS), BF16),
            pltpu.VMEM((8, FACE), jnp.int32),
            pltpu.VMEM((27 * C, C), BF16),
            pltpu.VMEM((27 * C, C), BF16),
            dma((6,)),
            pltpu.VMEM((2, 2, FACE, C), BF16),
            pltpu.VMEM((2, 2, FACE, C), BF16),
            dma((2, 2, 8)),
            dma((2, 2, 8)),
            pltpu.VMEM((8, FACE), jnp.int32),
            pltpu.VMEM((8, 8, FACE), jnp.int32),
            dma((8,)),
            dma((8,)),
            pltpu.VMEM((9, 96 * SLOTS, DATA), BF16),
            pltpu.VMEM((2, 2) + window, BF16),
            pltpu.VMEM((2, ROWS, C), BF16),
            pltpu.VMEM(window, BF16),
            pltpu.VMEM((ROWS, C), BF16),
            dma((4,)),
            pltpu.VMEM((C, 2 * ROWS), BF16),
            pltpu.VMEM((27 * C, C), F32),
        ]
        + reduce_scratch(nz),
        compiler_params=pltpu.CompilerParams(
            collective_id=0, has_side_effects=True, vmem_limit_bytes=LIMIT
        ),
        name="step",
    )(feat, cot, pick, table, coords, counts, first_weight, second_weight)
    results = (out, grad, first_grad, second_grad)
    out, grad, first_grad, second_grad = pl.pallas_call(
        store_kernel,
        out_shape=[struct(result.shape, F32) for result in results],
        in_specs=[hbm()] * 4,
        out_specs=[hbm()] * 4,
        scratch_shapes=[pltpu.VMEM(result.shape, F32) for result in results] + [dma((8,))],
        name="store",
    )(*results)
    return out.reshape(features.shape), grad.reshape(features.shape), first_grad.T, second_grad.T


def solution(mesh):
    placed = (
        P("gx", "gy", None, None, None),
        P("gx", "gy", None),
        P("gx", "gy"),
        P(),
        P(),
        P("gx", "gy", None, None, None),
    )
    return jax.shard_map(
        per_device,
        mesh=mesh,
        in_specs=placed,
        out_specs=(
            P("gx", "gy", None, None, None),
            P("gx", "gy", None, None, None),
            P("gx", "gy"),
            P("gx", "gy"),
        ),
        check_vma=False,
    )
```

```python
import functools
import math

import jax
import jax.numpy as jnp
import numpy as np
from jax import lax
from jax.experimental import pallas as pl
from jax.experimental.pallas import tpu as pltpu
from jax.sharding import PartitionSpec as P

C = 256
SLOTS = 3
ROWS = 192
FACE = 192
DATA = FACE + ROWS
DEAD = -(1 << 24)
LIMIT = 58 << 20
MESH = pl.DeviceIdType.MESH
F32 = jnp.float32
BF16 = jnp.bfloat16

REGIONS = (
    (-1, 0, 0, 32),
    (1, 0, 32, 32),
    (0, -1, 64, 32),
    (0, 1, 96, 32),
    (-1, -1, 128, 16),
    (-1, 1, 144, 16),
    (1, -1, 160, 16),
    (1, 1, 176, 16),
)


def face_tables():
    pick = np.zeros((2, FACE, ROWS), np.float32)
    table = np.zeros((8, DATA), np.int32)
    table[1] = DEAD
    for index, (sx, sy, start, count) in enumerate(REGIONS):
        xs = range(4) if sx == 0 else ((3,) if sx < 0 else (0,))
        ys = range(4) if sy == 0 else ((3,) if sy < 0 else (0,))
        row = start
        for slot in (0, 2):
            for vx in xs:
                for vy in ys:
                    for vz in range(4):
                        voxel = vx * 16 + vy * 4 + vz
                        pick[0, row, slot * 64 + voxel] = 1.0
                        pick[1, row, (slot or 1) * 64 + voxel] = 1.0
                        table[0, row] = slot
                        table[1, row] = (
                            (8 * sx + vx + 1) * 4096 + (8 * sy + vy + 1) * 64 + vz + 1
                        )
                        row += 1
        region = slice(start, start + count)
        table[2, region], table[3, region], table[4, region] = -sx, -sy, index
        table[5, region] = sx != 0
        table[6, region] = (sx or sy) < 0
    return pick, table


def block_codes(coords_ref, counts_ref):
    codes = []
    for slot in range(SLOTS):
        p = coords_ref[0, slot]
        code = (p // 16) * (4 * 4096) + ((p // 8) % 2) * (4 * 64) + (p % 8) * 4
        codes.append((code, slot < counts_ref[0, 0]))
    return codes


def by_slot(slot, codes):
    values = [jnp.where(live, code, DEAD) for code, live in codes]
    return jnp.where(slot == 0, values[0], jnp.where(slot == 1, values[1], values[2]))


def swap_faces(packed, landed, send_sems, recv_sems, index_last=False):
    copies = []
    for index, (peer, (_, _, start, count)) in enumerate(zip(around(), REGIONS)):
        part = pl.ds(start, count)
        copies.append(
            pltpu.make_async_remote_copy(
                src_ref=packed if index_last else packed.at[part],
                dst_ref=landed.at[index] if index_last else landed.at[part],
                send_sem=send_sems.at[index],
                recv_sem=recv_sems.at[index],
                device_id=peer,
                device_id_type=MESH,
            )
        )
    return copies


def around():
    nx, ny = lax.axis_size("gx"), lax.axis_size("gy")
    gx, gy = lax.axis_index("gx"), lax.axis_index("gy")
    return [
        (lax.rem(gx - sx + nx, nx), lax.rem(gy - sy + ny, ny)) for sx, sy, _, _ in REGIONS
    ]


def build_placing(code, coords_ref, placing):
    row = lax.broadcasted_iota(jnp.int32, (96, DATA), 0)
    pattern = (row // 16) * 4096 + ((row // 4) % 4) * 64 + row % 4
    offset = jnp.broadcast_to(code, (96, DATA)) - pattern
    for slot in range(SLOTS):
        p = coords_ref[0, slot]
        start = (p // 16) * (4 * 4096) + ((p // 8) % 2) * (4 * 64) + (p % 8) * 4
        for shift in range(9):
            placing[shift, slot * 96 : slot * 96 + 96, :] = jnp.where(
                offset == start + (shift // 3) * 64 + shift % 3, 1.0, 0.0
            ).astype(BF16)


def build_windows(landed, own, placing, win_ref):
    data = jnp.concatenate([landed, own], axis=0)
    for shift in range(9):
        rows = jnp.dot(placing[shift], data, preferred_element_type=F32).astype(BF16)
        win_ref[shift] = rows.reshape(SLOTS, 6, 16, C)


def tap_rows(win_ref, tap):
    return win_ref[tap % 9, :, tap // 9 : tap // 9 + 4].reshape(ROWS, C)


def conv(win_ref, weight_ref):
    total = jnp.zeros((ROWS, C), F32)
    for tap in range(27):
        total += jnp.dot(
            tap_rows(win_ref, tap),
            weight_ref[tap * C : (tap + 1) * C, :],
            preferred_element_type=F32,
        )
    return total


def conv_back(win_ref, weight_ref):
    total = jnp.zeros((ROWS, C), F32)
    for tap in range(27):
        total += lax.dot_general(
            tap_rows(win_ref, 26 - tap),
            weight_ref[tap * C : (tap + 1) * C, :],
            (((1,), (1,)), ((), ())),
            preferred_element_type=F32,
        )
    return total


def live_rows(counts_ref):
    return lax.broadcasted_iota(jnp.int32, (ROWS, C), 0) < counts_ref[0, 0] * 64


BLOCK = 216
TILES = 27
PACKED = 56


class Ring:
    def __init__(self, own, out, inbox, sends, recvs, me, peers, place, direct):
        self.own, self.out, self.inbox = own, out, inbox
        self.sends, self.recvs = sends, recvs
        self.me = place(me)
        self.to_right = place(lax.rem(me + 1, 4))
        self.to_left = place(lax.rem(me + 3, 4))
        across = place(lax.rem(me + 2, 4))
        right, left, self.far = peers
        self.half = own.shape[1] // 2
        self.direct = direct
        self.plan = (
            (across, self.half, right),
            (across, 0, left),
            (self.to_right, 0, right),
            (self.to_left, self.half, left),
            (self.to_right, self.half, right),
            (self.to_left, 0, left),
        )

    def copy(self, index, piece):
        target, base, peer = self.plan[index]
        if self.direct(piece) and index < 2:
            peer = self.far
        return pltpu.make_async_remote_copy(
            src_ref=self.out.at[target, base + piece],
            dst_ref=self.inbox.at[index, piece],
            send_sem=self.sends.at[index, piece],
            recv_sem=self.recvs.at[index, piece],
            device_id=peer,
            device_id_type=MESH,
        )

    def start(self, piece, upper):
        for index in (0, 3) if upper else (1, 2):
            self.copy(index, piece).start()
        if self.direct(piece):
            self.copy(4 if upper else 5, piece).start()

    def relay(self, piece):
        for index in () if self.direct(piece) else (0, 1):
            target, base, _ = self.plan[4 + index]
            self.copy(index, piece).wait_recv()
            total = self.own[target, base + piece] + self.inbox[index, piece].astype(F32)
            self.out[target, base + piece] = total.astype(BF16)
            self.copy(4 + index, piece).start()

    def arrive(self, piece):
        for index in range(0 if self.direct(piece) else 2, 6):
            self.copy(index, piece).wait_recv()

    def total(self, piece, upper):
        total = self.own[self.me, piece + self.half * upper]
        for index in (3, 4, 0) if upper else (2, 5, 1):
            if index > 1 or self.direct(piece):
                total += self.inbox[index, piece].astype(F32)
        return total

    def drain(self):
        for piece in range(self.half):
            for index in range(6):
                self.copy(index, piece).wait_send()


def ring_scratch(nz, rows):
    return [
        pltpu.VMEM((4, nz, rows, 128), F32),
        pltpu.VMEM((4, nz, rows, 128), BF16),
        pltpu.VMEM((6, nz // 2, rows, 128), BF16),
        pltpu.SemaphoreType.DMA((6, nz // 2)),
        pltpu.SemaphoreType.DMA((6, nz // 2)),
    ]


def reduce_scratch(nz):
    return (
        ring_scratch(nz, BLOCK) * 2
        + ring_scratch(nz, PACKED) * 2
        + [
            pltpu.VMEM((2, nz, PACKED, 128), F32),
            pltpu.VMEM((2, nz, PACKED, 128), F32),
            pltpu.VMEM((2, nz, PACKED, 128), BF16),
            pltpu.VMEM((2, nz, PACKED, 128), BF16),
            pltpu.VMEM((2, PACKED, 128), F32),
            pltpu.SemaphoreType.DMA((2, nz)),
            pltpu.SemaphoreType.DMA((2, nz)),
        ]
    )


def swapped(t):
    return lax.rem(t, 2) * 2 + t // 2


def straight(t):
    return t


def chip_place():
    gx, gy = lax.axis_index("gx"), lax.axis_index("gy")
    z, x, core, y = gx // 4, (lax.rem(gx, 4) // 2) * 2 + lax.rem(gy, 2), lax.rem(gx, 2), gy // 2
    return x, y, z, core


def device_at(x, y, z, core):
    return (z * 4 + (x // 2) * 2 + core, y * 2 + lax.rem(x, 2))


def reduce_peers(nz):
    x, y, z, core = chip_place()
    return (
        [device_at(x, y, z, 1 - core)]
        + [device_at(lax.rem(x + step, 4), y, z, core) for step in (1, 2, 3)]
        + [device_at(x, lax.rem(y + step, 4), z, core) for step in (1, 2, 3)]
        + [device_at(x, y, lax.rem(z + step, nz), c) for step in range(1, nz) for c in range(2)]
    )


def spread(rows, own, out, z):
    lane = lax.broadcasted_iota(jnp.int32, (8, 128), 1) // 32
    tiles = rows.reshape(TILES, 8, 128)
    for target in range(4):
        packed = []
        for group in range(7):
            tile = None
            for part in range(4):
                index = 4 * group + part
                if index >= TILES:
                    continue
                shift = (part - target) % 4 * 32
                moved = pltpu.roll(tiles[index], shift, 1) if shift else tiles[index]
                tile = moved if tile is None else jnp.where(lane == part, moved, tile)
            packed.append(tile)
        block = jnp.concatenate(packed, axis=0)
        own[target, z] = block
        out[target, z] = block.astype(BF16)


def unspread(packed):
    tiles = packed.reshape(7, 8, 128)
    rows = []
    for index in range(TILES):
        part = index % 4
        tile = tiles[index // 4]
        rows.append(pltpu.roll(tile, 128 - 32 * part, 1) if part else tile)
    rows += [jnp.zeros((8, 128), F32)] * (32 - TILES)
    return jnp.concatenate(rows, axis=0).T[:32, :BLOCK]


class Reduce:
    def __init__(self, nz, scale, term, scratch):
        self.nz, self.scale, self.term, self.half = nz, scale, term, nz // 2
        self.clock = 0
        self.x, self.y, self.z, self.core = chip_place()
        x, y, z, core = self.x, self.y, self.z, self.core
        xs, ys, ys2, xs2 = (scratch[5 * i : 5 * i + 5] for i in range(4))
        self.zown, self.zin, self.zout, self.zlate, self.last, self.zsend, self.zrecv = scratch[20:]
        along_x = [device_at(lax.rem(x + step, 4), y, z, core) for step in (1, 3, 2)]
        along_y = [device_at(x, lax.rem(y + step, 4), z, core) for step in (1, 3, 2)]

        def never(piece):
            return False

        def last(piece):
            return piece == self.half - 1

        self.firsts = [
            Ring(*xs, x, along_x, straight, never),
            Ring(*ys, y, along_y, straight, never),
        ]
        self.seconds = [
            Ring(*ys2, y, along_y, swapped, last),
            Ring(*xs2, x, along_x, straight, last),
        ]

    def advance(self):
        for stage, step in enumerate((self.relay, self.turn, self.turn_relay, self.along)):
            piece = self.clock - 1 - stage
            if 0 <= piece < self.half:
                step(piece)
        self.clock += 1
        return self.clock <= self.half + 4

    def begin(self, piece, upper):
        term, z = self.term, piece + upper * self.half
        lane = lax.broadcasted_iota(jnp.int32, (BLOCK, 128), 1)
        even = (lane // 32) % 2 == 0
        below = lane < 64

        def place(ring, target, value):
            ring.own[target, z] = value
            ring.out[target, z] = value.astype(BF16)

        ring = self.firsts[0]
        for half in range(2):
            start = (4 * z + 2 * half) * BLOCK
            left, right = term[start : start + BLOCK, :128], term[start : start + BLOCK, 128:]
            place(ring, 2 * half, jnp.where(even, left, pltpu.roll(right, 32, 1)))
            place(ring, 2 * half + 1, jnp.where(even, pltpu.roll(left, 96, 1), right))
        ring.start(piece, upper)
        ring = self.firsts[1]
        for pair in range(2):
            zero, one = (
                term[start : start + BLOCK, 128 * pair : 128 * pair + 128]
                for start in ((4 * z + 1) * BLOCK, (4 * z + 3) * BLOCK)
            )
            place(ring, 2 * pair, jnp.where(below, zero, pltpu.roll(one, 64, 1)))
            place(ring, 2 * pair + 1, jnp.where(below, pltpu.roll(zero, 64, 1), one))
        ring.start(piece, upper)

    def relay(self, piece):
        for ring in self.firsts:
            ring.relay(piece)

    def turn(self, piece):
        for ring, following in zip(self.firsts, self.seconds):
            ring.arrive(piece)
            for upper in range(2):
                spread(
                    ring.total(piece, upper),
                    following.own,
                    following.out,
                    piece + upper * self.half,
                )
                following.start(piece, upper)

    def turn_relay(self, piece):
        for ring in self.seconds:
            ring.relay(piece)

    def zcopy(self, color, to_z, source, slot):
        late = to_z % self.half == self.half - 1
        return pltpu.make_async_remote_copy(
            src_ref=(self.zout if late else self.zown).at[color, to_z],
            dst_ref=(self.zlate if late else self.zin).at[source, slot],
            send_sem=self.zsend.at[color, to_z],
            recv_sem=self.zrecv.at[source, slot],
            device_id=device_at(self.x, self.y, to_z, color),
            device_id_type=MESH,
        )

    def along(self, piece):
        for color, ring in enumerate(self.seconds):
            ring.arrive(piece)
            for upper in range(2):
                to_z = piece + upper * self.half
                total = ring.total(piece, upper)
                self.zown[color, to_z] = total
                if piece == self.half - 1:
                    self.zout[color, to_z] = total.astype(BF16)

                @pl.when((self.z != to_z) | (self.core != color))
                def _():
                    self.zcopy(color, to_z, self.core, self.z).start()

    def gather(self, late):
        inbox, to_z = (self.zlate, self.half - 1) if late else (self.zin, 0)
        for source in range(2):
            for from_z in range(self.nz):

                @pl.when((self.z != from_z) | (self.core != source))
                def _():
                    self.zcopy(0, to_z, source, from_z).wait_recv()
                    self.last[source] += inbox[source, from_z].astype(F32)

    def finish(self, first_ref, second_ref):
        self.last[self.core] = self.zown[self.core, self.z]
        self.last[1 - self.core] = jnp.zeros((PACKED, 128), F32)
        late = lax.rem(self.z, self.half) == self.half - 1

        @pl.when(late)
        def _():
            self.gather(True)

        @pl.when(jnp.logical_not(late))
        def _():
            self.gather(False)

        first_ref[...] = unspread(self.last[0] * self.scale)
        second_ref[...] = unspread(self.last[1] * self.scale)

    def drain(self):
        for ring in self.firsts + self.seconds:
            ring.drain()
        for color in range(2):
            for to_z in range(self.nz):

                @pl.when((self.z != to_z) | (self.core != color))
                def _():
                    self.zcopy(color, to_z, self.core, self.z).wait_send()


def gradient_taps(nz):
    done, steps = set(), []
    for piece in range(nz // 2):
        for upper in range(2):
            z = piece + upper * (nz // 2)
            taps = set(range(864 * z // C, -(-864 * (z + 1) // C)))
            steps.append((piece, upper, sorted(taps - done)))
            done |= taps
    return steps


def runs(taps):
    out = []
    for tap in taps:
        if out and out[-1][1] == tap:
            out[-1][1] = tap + 1
        else:
            out.append([tap, tap + 1])
    return out


def step_kernel(
    nz,
    scale,
    feat_hbm,
    cot_hbm,
    pick_hbm,
    table_hbm,
    coords_ref,
    counts_ref,
    w1_hbm,
    w2_hbm,
    out_hbm,
    grad_hbm,
    first_hbm,
    second_hbm,
    out_ref,
    grad_ref,
    first_ref,
    second_ref,
    put_sems,
    feat,
    cot,
    picks,
    pick,
    table,
    w1,
    w2,
    load_sems,
    packed,
    landed,
    send_sems,
    recv_sems,
    sent_code,
    codes_in,
    code_send,
    code_recv,
    placing,
    win,
    rows,
    pair_win,
    pair_rows,
    pair_sems,
    turned,
    term,
    *scratch,
):
    nx, ny = lax.axis_size("gx"), lax.axis_size("gy")
    gx, gy = lax.axis_index("gx"), lax.axis_index("gy")
    x, y, z, core = chip_place()
    peers = around() + reduce_peers(nz)
    barrier = pltpu.get_barrier_semaphore()
    for peer in peers:
        pl.semaphore_signal(barrier, inc=1, device_id=peer, device_id_type=MESH)
    loads = [
        pltpu.make_async_copy(source, target, load_sems.at[index])
        for index, (source, target) in enumerate(
            (
                (feat_hbm, feat),
                (cot_hbm, cot),
                (pick_hbm, picks),
                (table_hbm, table),
                (w1_hbm, w1),
                (w2_hbm, w2),
            )
        )
    ]
    for load in loads:
        load.start()
    for load in loads[:4]:
        load.wait()
    blocks = block_codes(coords_ref, counts_ref)
    to_x = gx + table[2:3, :]
    to_y = gy + table[3:4, :]
    inside = (to_x >= 0) & (to_x < nx) & (to_y >= 0) & (to_y < ny)
    corner = coords_ref[0, 0] // 8
    side = jnp.where(table[5:6, :] == 1, corner // 2, corner % 2)
    ground = jnp.where(side == table[6:7, :], 0, 1)
    sent = table[1:2, :] + by_slot(jnp.where(table[0:1, :] == 2, 2, ground), blocks)
    for sx, sy, start, count in REGIONS:
        first = (corner // 2 if sx else corner % 2) == (1 if (sx or sy) < 0 else 0)
        part = slice(start, start + count)
        pick[part] = jnp.where(first, picks[0, part], picks[1, part])
    sent_code[...] = jnp.broadcast_to(jnp.where(inside, sent, DEAD), (8, DATA))
    packed[0, 0] = jnp.dot(pick[...], feat[...], preferred_element_type=F32).astype(BF16)
    packed[0, 1] = jnp.dot(pick[...], cot[...], preferred_element_type=F32).astype(BF16)
    faces = [
        swap_faces(
            packed.at[phase, field],
            landed.at[phase, field],
            send_sems.at[phase, field],
            recv_sems.at[phase, field],
        )
        for phase in range(2)
        for field in range(2)
    ]
    code_copies = swap_faces(sent_code, codes_in, code_send, code_recv, True)
    pl.semaphore_wait(barrier, len(peers))
    for copy in code_copies + faces[0] + faces[1]:
        copy.start()
    lane = lax.broadcasted_iota(jnp.int32, (8, DATA), 1)
    voxel = lane % 64
    own = (voxel // 16 + 1) * 4096 + ((voxel // 4) % 4 + 1) * 64 + voxel % 4 + 1
    own += by_slot(lane // 64 - FACE // 64, blocks)
    live = live_rows(counts_ref)
    region = jnp.broadcast_to(table[4:5, :], (8, DATA))
    for copy in code_copies:
        copy.wait_recv()
    got = codes_in[0]
    for index in range(1, 8):
        got = jnp.where(region == index, codes_in[index], got)
    code = jnp.where(lane < FACE, got, own)[0:1, :]
    build_placing(code, coords_ref, placing)
    for copy in faces[0]:
        copy.wait_recv()
    build_windows(landed[0, 0], feat[...], placing, win.at[0, 0])
    pair = [
        pltpu.make_async_remote_copy(
            src_ref=source,
            dst_ref=target,
            send_sem=pair_sems.at[2 * index],
            recv_sem=pair_sems.at[2 * index + 1],
            device_id=device_at(x, y, z, 1 - core),
            device_id_type=MESH,
        )
        for index, (source, target) in enumerate(
            ((win.at[0, 1 - core], pair_win), (rows.at[core], pair_rows))
        )
    ]
    loads[4].wait()
    pre = conv(win.at[0, 0], w1)
    gate = jax.nn.sigmoid(pre)
    hidden = jnp.where(live, pre * gate, 0.0).astype(BF16)
    rows[0] = hidden
    packed[1, 0] = jnp.dot(pick[...], hidden, preferred_element_type=F32).astype(BF16)
    for copy in faces[1]:
        copy.wait_recv()
    build_windows(landed[0, 1], cot[...], placing, win.at[0, 1])
    pair[0].start()
    loads[5].wait()
    hidden_grad = conv_back(win.at[0, 1], w2)
    pre_grad = jnp.where(live, hidden_grad * gate * (1.0 + pre * (1.0 - gate)), 0.0).astype(BF16)
    rows[1] = pre_grad
    packed[1, 1] = jnp.dot(pick[...], pre_grad, preferred_element_type=F32).astype(BF16)
    pair[1].start()
    for copy in faces[2] + faces[3]:
        copy.start()
    for copy in pair:
        copy.wait_recv()

    def window(tap):
        shift, start = lax.rem(tap, 9), tap // 9
        return jnp.concatenate(
            [
                win[0, core, shift, :, pl.ds(start, 4)].reshape(ROWS, C),
                pair_win[shift, :, pl.ds(start, 4)].reshape(ROWS, C),
            ],
            axis=0,
        )

    both = jnp.concatenate([rows[1 - core], pair_rows[...]], axis=0)
    turned[...] = both.astype(F32).T.astype(BF16)
    reduce = Reduce(nz, scale, term, scratch)
    for piece, upper, taps in gradient_taps(nz):
        for start, stop in runs(taps):

            @pl.when(core == 0)
            def _():
                @pl.loop(start, stop)
                def _(tap):
                    term[pl.ds(pl.multiple_of(tap * C, C), C), :] = lax.dot_general(
                        window(tap),
                        jnp.concatenate([rows[1], pair_rows[...]], axis=0),
                        (((0,), (0,)), ((), ())),
                        preferred_element_type=F32,
                    )

            @pl.when(core == 1)
            def _():
                @pl.loop(start, stop)
                def _(tap):
                    term[pl.ds(pl.multiple_of(tap * C, C), C), :] = jnp.dot(
                        turned[...], window(26 - tap), preferred_element_type=F32
                    )

        reduce.begin(piece, upper)
        if upper:
            reduce.advance()
    for field in range(2):
        for copy in faces[2 + field]:
            copy.wait_recv()
        build_windows(landed[1, field], rows[field], placing, win.at[1, field])
    reduce.advance()
    out_ref[...] = jnp.where(live, conv(win.at[1, 0], w2), 0.0)
    puts = [
        pltpu.make_async_copy(source, target, put_sems.at[index])
        for index, (source, target) in enumerate(
            (
                (out_ref, out_hbm),
                (grad_ref, grad_hbm),
                (first_ref, first_hbm),
                (second_ref, second_hbm),
            )
        )
    ]
    puts[0].start()
    reduce.advance()
    grad_ref[...] = jnp.where(live, conv_back(win.at[1, 1], w1), 0.0)
    puts[1].start()
    while reduce.advance():
        pass
    reduce.finish(first_ref, second_ref)
    for put in puts[2:]:
        put.start()
    for copy in code_copies + sum(faces, []) + pair:
        copy.wait_send()
    reduce.drain()
    for put in puts:
        put.wait()


def store_kernel(*refs):
    sources, targets, held, sems = refs[:4], refs[4:8], refs[8:12], refs[12]
    takes = [
        pltpu.make_async_copy(sources[index], held[index], sems.at[index]) for index in range(4)
    ]
    puts = [
        pltpu.make_async_copy(held[index], targets[index], sems.at[4 + index])
        for index in range(4)
    ]
    for take in takes:
        take.start()
    for take, put in zip(takes, puts):
        take.wait()
        put.start()
    for put in puts:
        put.wait()


def vmem():
    return pl.BlockSpec(memory_space=pltpu.VMEM)


def smem():
    return pl.BlockSpec(memory_space=pltpu.SMEM)


def hbm():
    return pl.BlockSpec(memory_space=pltpu.HBM)


def per_device(features, block_coords, block_counts, first_weight, second_weight, cotangent):
    feat = features.reshape(ROWS, C)
    cot = cotangent.reshape(ROWS, C)
    coords = block_coords.reshape(1, SLOTS)
    counts = block_counts.reshape(1, 1)
    pick_np, table_np = face_tables()
    pick = jnp.asarray(pick_np, BF16)
    table = jnp.asarray(table_np)
    struct = jax.ShapeDtypeStruct
    scale = 1.0 / math.sqrt(64 * SLOTS * lax.axis_size("gx") * lax.axis_size("gy"))
    nz = lax.axis_size("gx") // 4
    window = (9, SLOTS, 6, 16, C)
    dma = pltpu.SemaphoreType.DMA
    out, grad, first_grad, second_grad = pl.pallas_call(
        functools.partial(step_kernel, nz, scale),
        out_shape=(
            struct((ROWS, C), F32),
            struct((ROWS, C), F32),
            struct((32, BLOCK), F32),
            struct((32, BLOCK), F32),
        ),
        in_specs=[hbm()] * 4 + [smem()] * 2 + [hbm()] * 2,
        out_specs=(hbm(),) * 4,
        scratch_shapes=[
            pltpu.VMEM((ROWS, C), F32),
            pltpu.VMEM((ROWS, C), F32),
            pltpu.VMEM((32, BLOCK), F32),
            pltpu.VMEM((32, BLOCK), F32),
            dma((4,)),
            pltpu.VMEM((ROWS, C), BF16),
            pltpu.VMEM((ROWS, C), BF16),
            pltpu.VMEM((2, FACE, ROWS), BF16),
            pltpu.VMEM((FACE, ROWS), BF16),
            pltpu.VMEM((8, DATA), jnp.int32),
            pltpu.VMEM((27 * C, C), BF16),
            pltpu.VMEM((27 * C, C), BF16),
            dma((6,)),
            pltpu.VMEM((2, 2, FACE, C), BF16),
            pltpu.VMEM((2, 2, FACE, C), BF16),
            dma((2, 2, 8)),
            dma((2, 2, 8)),
            pltpu.VMEM((8, DATA), jnp.int32),
            pltpu.VMEM((8, 8, DATA), jnp.int32),
            dma((8,)),
            dma((8,)),
            pltpu.VMEM((9, 96 * SLOTS, DATA), BF16),
            pltpu.VMEM((2, 2) + window, BF16),
            pltpu.VMEM((2, ROWS, C), BF16),
            pltpu.VMEM(window, BF16),
            pltpu.VMEM((ROWS, C), BF16),
            dma((4,)),
            pltpu.VMEM((C, 2 * ROWS), BF16),
            pltpu.VMEM((27 * C, C), F32),
        ]
        + reduce_scratch(nz),
        compiler_params=pltpu.CompilerParams(
            collective_id=0, has_side_effects=True, vmem_limit_bytes=LIMIT
        ),
        name="step",
    )(feat, cot, pick, table, coords, counts, first_weight, second_weight)
    results = (out, grad, first_grad, second_grad)
    out, grad, first_grad, second_grad = pl.pallas_call(
        store_kernel,
        out_shape=[struct(result.shape, F32) for result in results],
        in_specs=[hbm()] * 4,
        out_specs=[hbm()] * 4,
        scratch_shapes=[pltpu.VMEM(result.shape, F32) for result in results] + [dma((8,))],
        name="store",
    )(*results)
    return out.reshape(features.shape), grad.reshape(features.shape), first_grad.T, second_grad.T


def solution(mesh):
    placed = (
        P("gx", "gy", None, None, None),
        P("gx", "gy", None),
        P("gx", "gy"),
        P(),
        P(),
        P("gx", "gy", None, None, None),
    )
    return jax.shard_map(
        per_device,
        mesh=mesh,
        in_specs=placed,
        out_specs=(
            P("gx", "gy", None, None, None),
            P("gx", "gy", None, None, None),
            P("gx", "gy"),
            P("gx", "gy"),
        ),
        check_vma=False,
    )
```

```python
import functools
import math

import jax
import jax.numpy as jnp
import numpy as np
from jax import lax
from jax.experimental import pallas as pl
from jax.experimental.pallas import tpu as pltpu
from jax.sharding import PartitionSpec as P

C = 256
SLOTS = 3
ROWS = 192
FACE = 192
DATA = FACE + ROWS
DEAD = -(1 << 24)
LIMIT = 58 << 20
MESH = pl.DeviceIdType.MESH
F32 = jnp.float32
BF16 = jnp.bfloat16

REGIONS = (
    (-1, 0, 0, 32),
    (1, 0, 32, 32),
    (0, -1, 64, 32),
    (0, 1, 96, 32),
    (-1, -1, 128, 16),
    (-1, 1, 144, 16),
    (1, -1, 160, 16),
    (1, 1, 176, 16),
)


def face_tables():
    pick = np.zeros((2, FACE, ROWS), np.float32)
    table = np.zeros((8, DATA), np.int32)
    table[1] = DEAD
    for index, (sx, sy, start, count) in enumerate(REGIONS):
        xs = range(4) if sx == 0 else ((3,) if sx < 0 else (0,))
        ys = range(4) if sy == 0 else ((3,) if sy < 0 else (0,))
        row = start
        for slot in (0, 2):
            for vx in xs:
                for vy in ys:
                    for vz in range(4):
                        voxel = vx * 16 + vy * 4 + vz
                        pick[0, row, slot * 64 + voxel] = 1.0
                        pick[1, row, (slot or 1) * 64 + voxel] = 1.0
                        table[0, row] = slot
                        table[1, row] = (
                            (8 * sx + vx + 1) * 4096 + (8 * sy + vy + 1) * 64 + vz + 1
                        )
                        row += 1
        region = slice(start, start + count)
        table[2, region], table[3, region], table[4, region] = -sx, -sy, index
        table[5, region] = sx != 0
        table[6, region] = (sx or sy) < 0
    return pick, table


def block_codes(coords_ref, counts_ref):
    codes = []
    for slot in range(SLOTS):
        p = coords_ref[0, slot]
        code = (p // 16) * (4 * 4096) + ((p // 8) % 2) * (4 * 64) + (p % 8) * 4
        codes.append((code, slot < counts_ref[0, 0]))
    return codes


def by_slot(slot, codes):
    values = [jnp.where(live, code, DEAD) for code, live in codes]
    return jnp.where(slot == 0, values[0], jnp.where(slot == 1, values[1], values[2]))


def swap_faces(packed, landed, send_sems, recv_sems, index_last=False):
    copies = []
    for index, (peer, (_, _, start, count)) in enumerate(zip(around(), REGIONS)):
        part = pl.ds(start, count)
        copies.append(
            pltpu.make_async_remote_copy(
                src_ref=packed if index_last else packed.at[part],
                dst_ref=landed.at[index] if index_last else landed.at[part],
                send_sem=send_sems.at[index],
                recv_sem=recv_sems.at[index],
                device_id=peer,
                device_id_type=MESH,
            )
        )
    return copies


def around():
    nx, ny = lax.axis_size("gx"), lax.axis_size("gy")
    gx, gy = lax.axis_index("gx"), lax.axis_index("gy")
    return [
        (lax.rem(gx - sx + nx, nx), lax.rem(gy - sy + ny, ny)) for sx, sy, _, _ in REGIONS
    ]


def build_placing(code, coords_ref, placing):
    row = lax.broadcasted_iota(jnp.int32, (96, DATA), 0)
    pattern = (row // 16) * 4096 + ((row // 4) % 4) * 64 + row % 4
    offset = jnp.broadcast_to(code, (96, DATA)) - pattern
    for slot in range(SLOTS):
        p = coords_ref[0, slot]
        start = (p // 16) * (4 * 4096) + ((p // 8) % 2) * (4 * 64) + (p % 8) * 4
        for shift in range(9):
            placing[shift, slot * 96 : slot * 96 + 96, :] = jnp.where(
                offset == start + (shift // 3) * 64 + shift % 3, 1.0, 0.0
            ).astype(BF16)


def build_windows(landed, own, placing, win_ref):
    data = jnp.concatenate([landed, own], axis=0)
    for shift in range(9):
        rows = jnp.dot(placing[shift], data, preferred_element_type=F32).astype(BF16)
        win_ref[shift] = rows.reshape(SLOTS, 6, 16, C)


def tap_rows(win_ref, tap):
    return win_ref[tap % 9, :, tap // 9 : tap // 9 + 4].reshape(ROWS, C)


def conv(win_ref, weight_ref):
    total = jnp.zeros((ROWS, C), F32)
    for tap in range(27):
        total += jnp.dot(
            tap_rows(win_ref, tap),
            weight_ref[tap * C : (tap + 1) * C, :],
            preferred_element_type=F32,
        )
    return total


def conv_back(win_ref, weight_ref):
    total = jnp.zeros((ROWS, C), F32)
    for tap in range(27):
        total += lax.dot_general(
            tap_rows(win_ref, 26 - tap),
            weight_ref[tap * C : (tap + 1) * C, :],
            (((1,), (1,)), ((), ())),
            preferred_element_type=F32,
        )
    return total


def live_rows(counts_ref):
    return lax.broadcasted_iota(jnp.int32, (ROWS, C), 0) < counts_ref[0, 0] * 64


BLOCK = 216
TILES = 27
PACKED = 56


class Ring:
    def __init__(self, own, out, inbox, sends, recvs, me, peers, place, direct):
        self.own, self.out, self.inbox = own, out, inbox
        self.sends, self.recvs = sends, recvs
        self.me = place(me)
        self.to_right = place(lax.rem(me + 1, 4))
        self.to_left = place(lax.rem(me + 3, 4))
        across = place(lax.rem(me + 2, 4))
        right, left, self.far = peers
        self.half = own.shape[1] // 2
        self.direct = direct
        self.plan = (
            (across, self.half, right),
            (across, 0, left),
            (self.to_right, 0, right),
            (self.to_left, self.half, left),
            (self.to_right, self.half, right),
            (self.to_left, 0, left),
        )

    def copy(self, index, piece):
        target, base, peer = self.plan[index]
        if self.direct(piece) and index < 2:
            peer = self.far
        return pltpu.make_async_remote_copy(
            src_ref=self.out.at[target, base + piece],
            dst_ref=self.inbox.at[index, piece],
            send_sem=self.sends.at[index, piece],
            recv_sem=self.recvs.at[index, piece],
            device_id=peer,
            device_id_type=MESH,
        )

    def start(self, piece, upper):
        for index in (0, 3) if upper else (1, 2):
            self.copy(index, piece).start()
        if self.direct(piece):
            self.copy(4 if upper else 5, piece).start()

    def relay(self, piece, indices=(1, 0)):
        for index in () if self.direct(piece) else indices:
            target, base, _ = self.plan[4 + index]
            self.copy(index, piece).wait_recv()
            total = self.own[target, base + piece] + self.inbox[index, piece].astype(F32)
            self.out[target, base + piece] = total.astype(BF16)
            self.copy(4 + index, piece).start()

    def arrive(self, piece):
        for index in range(0 if self.direct(piece) else 2, 6):
            self.copy(index, piece).wait_recv()

    def total(self, piece, upper):
        total = self.own[self.me, piece + self.half * upper]
        for index in (3, 4, 0) if upper else (2, 5, 1):
            if index > 1 or self.direct(piece):
                total += self.inbox[index, piece].astype(F32)
        return total

    def drain(self):
        for piece in range(self.half):
            for index in range(6):
                self.copy(index, piece).wait_send()


def ring_scratch(nz, rows):
    return [
        pltpu.VMEM((4, nz, rows, 128), F32),
        pltpu.VMEM((4, nz, rows, 128), BF16),
        pltpu.VMEM((6, nz // 2, rows, 128), BF16),
        pltpu.SemaphoreType.DMA((6, nz // 2)),
        pltpu.SemaphoreType.DMA((6, nz // 2)),
    ]


def reduce_scratch(nz):
    return (
        ring_scratch(nz, BLOCK) * 2
        + ring_scratch(nz, PACKED) * 2
        + [
            pltpu.VMEM((2, nz, PACKED, 128), F32),
            pltpu.VMEM((2, nz, PACKED, 128), F32),
            pltpu.VMEM((2, nz, PACKED, 128), BF16),
            pltpu.VMEM((2, nz, PACKED, 128), BF16),
            pltpu.VMEM((2, PACKED, 128), F32),
            pltpu.SemaphoreType.DMA((2, nz)),
            pltpu.SemaphoreType.DMA((2, nz)),
        ]
    )


def swapped(t):
    return lax.rem(t, 2) * 2 + t // 2


def straight(t):
    return t


def chip_place():
    gx, gy = lax.axis_index("gx"), lax.axis_index("gy")
    z, x, core, y = gx // 4, (lax.rem(gx, 4) // 2) * 2 + lax.rem(gy, 2), lax.rem(gx, 2), gy // 2
    return x, y, z, core


def device_at(x, y, z, core):
    return (z * 4 + (x // 2) * 2 + core, y * 2 + lax.rem(x, 2))


def reduce_peers(nz):
    x, y, z, core = chip_place()
    return (
        [device_at(x, y, z, 1 - core)]
        + [device_at(lax.rem(x + step, 4), y, z, core) for step in (1, 2, 3)]
        + [device_at(x, lax.rem(y + step, 4), z, core) for step in (1, 2, 3)]
        + [device_at(x, y, lax.rem(z + step, nz), c) for step in range(1, nz) for c in range(2)]
    )


def spread(rows, own, out, z):
    lane = lax.broadcasted_iota(jnp.int32, (8, 128), 1) // 32
    tiles = rows.reshape(TILES, 8, 128)
    for target in range(4):
        packed = []
        for group in range(7):
            tile = None
            for part in range(4):
                index = 4 * group + part
                if index >= TILES:
                    continue
                shift = (part - target) % 4 * 32
                moved = pltpu.roll(tiles[index], shift, 1) if shift else tiles[index]
                tile = moved if tile is None else jnp.where(lane == part, moved, tile)
            packed.append(tile)
        block = jnp.concatenate(packed, axis=0)
        own[target, z] = block
        out[target, z] = block.astype(BF16)


def unspread(packed):
    tiles = packed.reshape(7, 8, 128)
    rows = []
    for index in range(TILES):
        part = index % 4
        tile = tiles[index // 4]
        rows.append(pltpu.roll(tile, 128 - 32 * part, 1) if part else tile)
    rows += [jnp.zeros((8, 128), F32)] * (32 - TILES)
    return jnp.concatenate(rows, axis=0).T[:32, :BLOCK]


class Reduce:
    def __init__(self, nz, scale, term, scratch):
        self.nz, self.scale, self.term, self.half = nz, scale, term, nz // 2
        self.clock = 0
        self.x, self.y, self.z, self.core = chip_place()
        x, y, z, core = self.x, self.y, self.z, self.core
        xs, ys, ys2, xs2 = (scratch[5 * i : 5 * i + 5] for i in range(4))
        self.zown, self.zin, self.zout, self.zlate, self.last, self.zsend, self.zrecv = scratch[20:]
        along_x = [device_at(lax.rem(x + step, 4), y, z, core) for step in (1, 3, 2)]
        along_y = [device_at(x, lax.rem(y + step, 4), z, core) for step in (1, 3, 2)]

        def never(piece):
            return False

        def last(piece):
            return piece == self.half - 1

        self.firsts = [
            Ring(*xs, x, along_x, straight, never),
            Ring(*ys, y, along_y, straight, never),
        ]
        self.seconds = [
            Ring(*ys2, y, along_y, swapped, last),
            Ring(*xs2, x, along_x, straight, last),
        ]

    def advance(self):
        for stage, step in enumerate((self.relay, self.turn, self.turn_relay, self.along)):
            piece = self.clock - 1 - stage
            if 0 <= piece < self.half:
                step(piece)
        self.clock += 1
        return self.clock <= self.half + 4

    def begin(self, piece, upper):
        term, z = self.term, piece + upper * self.half
        lane = lax.broadcasted_iota(jnp.int32, (BLOCK, 128), 1)
        even = (lane // 32) % 2 == 0
        below = lane < 64

        def place(ring, target, value):
            ring.own[target, z] = value
            ring.out[target, z] = value.astype(BF16)

        ring = self.firsts[0]
        for half in range(2):
            start = (4 * z + 2 * half) * BLOCK
            left, right = term[start : start + BLOCK, :128], term[start : start + BLOCK, 128:]
            place(ring, 2 * half, jnp.where(even, left, pltpu.roll(right, 32, 1)))
            place(ring, 2 * half + 1, jnp.where(even, pltpu.roll(left, 96, 1), right))
        ring.start(piece, upper)
        ring = self.firsts[1]
        for pair in range(2):
            zero, one = (
                term[start : start + BLOCK, 128 * pair : 128 * pair + 128]
                for start in ((4 * z + 1) * BLOCK, (4 * z + 3) * BLOCK)
            )
            place(ring, 2 * pair, jnp.where(below, zero, pltpu.roll(one, 64, 1)))
            place(ring, 2 * pair + 1, jnp.where(below, pltpu.roll(zero, 64, 1), one))
        ring.start(piece, upper)

    def relay_lower(self, piece):
        for ring in self.firsts:
            ring.relay(piece, (1,))

    def relay(self, piece):
        if piece == self.half - 1:
            self.relay_lower(piece)
        for ring in self.firsts:
            ring.relay(piece, (0,))

    def turn(self, piece):
        for ring, following in zip(self.firsts, self.seconds):
            ring.arrive(piece)
            for upper in range(2):
                spread(
                    ring.total(piece, upper),
                    following.own,
                    following.out,
                    piece + upper * self.half,
                )
                following.start(piece, upper)

    def turn_relay(self, piece):
        for ring in self.seconds:
            ring.relay(piece)

    def zcopy(self, color, to_z, source, slot):
        late = to_z % self.half == self.half - 1
        return pltpu.make_async_remote_copy(
            src_ref=(self.zout if late else self.zown).at[color, to_z],
            dst_ref=(self.zlate if late else self.zin).at[source, slot],
            send_sem=self.zsend.at[color, to_z],
            recv_sem=self.zrecv.at[source, slot],
            device_id=device_at(self.x, self.y, to_z, color),
            device_id_type=MESH,
        )

    def along(self, piece):
        for color, ring in enumerate(self.seconds):
            ring.arrive(piece)
            for upper in range(2):
                to_z = piece + upper * self.half
                total = ring.total(piece, upper)
                self.zown[color, to_z] = total
                if piece == self.half - 1:
                    self.zout[color, to_z] = total.astype(BF16)

                @pl.when((self.z != to_z) | (self.core != color))
                def _():
                    self.zcopy(color, to_z, self.core, self.z).start()

    def gather(self, late):
        inbox, to_z = (self.zlate, self.half - 1) if late else (self.zin, 0)
        for source in range(2):
            for from_z in range(self.nz):

                @pl.when((self.z != from_z) | (self.core != source))
                def _():
                    self.zcopy(0, to_z, source, from_z).wait_recv()
                    self.last[source] += inbox[source, from_z].astype(F32)

    def finish(self, first_ref, second_ref):
        self.last[self.core] = self.zown[self.core, self.z]
        self.last[1 - self.core] = jnp.zeros((PACKED, 128), F32)
        late = lax.rem(self.z, self.half) == self.half - 1

        @pl.when(late)
        def _():
            self.gather(True)

        @pl.when(jnp.logical_not(late))
        def _():
            self.gather(False)

        first_ref[...] = unspread(self.last[0] * self.scale)
        second_ref[...] = unspread(self.last[1] * self.scale)

    def drain(self):
        for ring in self.firsts + self.seconds:
            ring.drain()
        for color in range(2):
            for to_z in range(self.nz):

                @pl.when((self.z != to_z) | (self.core != color))
                def _():
                    self.zcopy(color, to_z, self.core, self.z).wait_send()


def gradient_taps(nz):
    done, steps = set(), []
    for piece in range(nz // 2):
        for upper in range(2):
            z = piece + upper * (nz // 2)
            taps = set(range(864 * z // C, -(-864 * (z + 1) // C)))
            steps.append((piece, upper, sorted(taps - done)))
            done |= taps
    return steps


def runs(taps):
    out = []
    for tap in taps:
        if out and out[-1][1] == tap:
            out[-1][1] = tap + 1
        else:
            out.append([tap, tap + 1])
    return out


def step_kernel(
    nz,
    scale,
    feat_hbm,
    cot_hbm,
    pick_hbm,
    table_hbm,
    coords_ref,
    counts_ref,
    w1_hbm,
    w2_hbm,
    out_hbm,
    grad_hbm,
    first_hbm,
    second_hbm,
    out_ref,
    grad_ref,
    first_ref,
    second_ref,
    put_sems,
    feat,
    cot,
    picks,
    pick,
    table,
    w1,
    w2,
    load_sems,
    packed,
    landed,
    send_sems,
    recv_sems,
    sent_code,
    codes_in,
    code_send,
    code_recv,
    placing,
    win,
    rows,
    pair_win,
    pair_rows,
    pair_sems,
    turned,
    term,
    *scratch,
):
    nx, ny = lax.axis_size("gx"), lax.axis_size("gy")
    gx, gy = lax.axis_index("gx"), lax.axis_index("gy")
    x, y, z, core = chip_place()
    peers = around() + reduce_peers(nz)
    barrier = pltpu.get_barrier_semaphore()
    for peer in peers:
        pl.semaphore_signal(barrier, inc=1, device_id=peer, device_id_type=MESH)
    loads = [
        pltpu.make_async_copy(source, target, load_sems.at[index])
        for index, (source, target) in enumerate(
            (
                (feat_hbm, feat),
                (cot_hbm, cot),
                (pick_hbm, picks),
                (table_hbm, table),
                (w1_hbm, w1),
                (w2_hbm, w2),
            )
        )
    ]
    for load in loads:
        load.start()
    for load in loads[:4]:
        load.wait()
    blocks = block_codes(coords_ref, counts_ref)
    to_x = gx + table[2:3, :]
    to_y = gy + table[3:4, :]
    inside = (to_x >= 0) & (to_x < nx) & (to_y >= 0) & (to_y < ny)
    corner = coords_ref[0, 0] // 8
    side = jnp.where(table[5:6, :] == 1, corner // 2, corner % 2)
    ground = jnp.where(side == table[6:7, :], 0, 1)
    sent = table[1:2, :] + by_slot(jnp.where(table[0:1, :] == 2, 2, ground), blocks)
    for sx, sy, start, count in REGIONS:
        first = (corner // 2 if sx else corner % 2) == (1 if (sx or sy) < 0 else 0)
        part = slice(start, start + count)
        pick[part] = jnp.where(first, picks[0, part], picks[1, part])
    sent_code[...] = jnp.broadcast_to(jnp.where(inside, sent, DEAD), (8, DATA))
    packed[0, 0] = jnp.dot(pick[...], feat[...], preferred_element_type=F32).astype(BF16)
    packed[0, 1] = jnp.dot(pick[...], cot[...], preferred_element_type=F32).astype(BF16)
    faces = [
        swap_faces(
            packed.at[phase, field],
            landed.at[phase, field],
            send_sems.at[phase, field],
            recv_sems.at[phase, field],
        )
        for phase in range(2)
        for field in range(2)
    ]
    code_copies = swap_faces(sent_code, codes_in, code_send, code_recv, True)
    pl.semaphore_wait(barrier, len(peers))
    for copy in code_copies + faces[0] + faces[1]:
        copy.start()
    lane = lax.broadcasted_iota(jnp.int32, (8, DATA), 1)
    voxel = lane % 64
    own = (voxel // 16 + 1) * 4096 + ((voxel // 4) % 4 + 1) * 64 + voxel % 4 + 1
    own += by_slot(lane // 64 - FACE // 64, blocks)
    live = live_rows(counts_ref)
    region = jnp.broadcast_to(table[4:5, :], (8, DATA))
    for copy in code_copies:
        copy.wait_recv()
    got = codes_in[0]
    for index in range(1, 8):
        got = jnp.where(region == index, codes_in[index], got)
    code = jnp.where(lane < FACE, got, own)[0:1, :]
    build_placing(code, coords_ref, placing)
    for copy in faces[0]:
        copy.wait_recv()
    build_windows(landed[0, 0], feat[...], placing, win.at[0, 0])
    pair = [
        pltpu.make_async_remote_copy(
            src_ref=source,
            dst_ref=target,
            send_sem=pair_sems.at[2 * index],
            recv_sem=pair_sems.at[2 * index + 1],
            device_id=device_at(x, y, z, 1 - core),
            device_id_type=MESH,
        )
        for index, (source, target) in enumerate(
            ((win.at[0, 1 - core], pair_win), (rows.at[core], pair_rows))
        )
    ]
    loads[4].wait()
    pre = conv(win.at[0, 0], w1)
    gate = jax.nn.sigmoid(pre)
    hidden = jnp.where(live, pre * gate, 0.0).astype(BF16)
    rows[0] = hidden

    @pl.when(core == 0)
    def _():
        pair[1].start()

    packed[1, 0] = jnp.dot(pick[...], hidden, preferred_element_type=F32).astype(BF16)
    for copy in faces[1]:
        copy.wait_recv()
    build_windows(landed[0, 1], cot[...], placing, win.at[0, 1])
    pair[0].start()
    loads[5].wait()
    hidden_grad = conv_back(win.at[0, 1], w2)
    pre_grad = jnp.where(live, hidden_grad * gate * (1.0 + pre * (1.0 - gate)), 0.0).astype(BF16)
    rows[1] = pre_grad

    @pl.when(core == 1)
    def _():
        pair[1].start()

    packed[1, 1] = jnp.dot(pick[...], pre_grad, preferred_element_type=F32).astype(BF16)
    for copy in faces[2] + faces[3]:
        copy.start()
    for copy in pair:
        copy.wait_recv()

    def window(tap):
        shift, start = lax.rem(tap, 9), tap // 9
        return jnp.concatenate(
            [
                win[0, core, shift, :, pl.ds(start, 4)].reshape(ROWS, C),
                pair_win[shift, :, pl.ds(start, 4)].reshape(ROWS, C),
            ],
            axis=0,
        )

    both = jnp.concatenate([rows[1 - core], pair_rows[...]], axis=0)
    turned[...] = both.astype(F32).T.astype(BF16)
    reduce = Reduce(nz, scale, term, scratch)
    for piece, upper, taps in gradient_taps(nz):
        for start, stop in runs(taps):

            @pl.when(core == 0)
            def _():
                @pl.loop(start, stop)
                def _(tap):
                    term[pl.ds(pl.multiple_of(tap * C, C), C), :] = lax.dot_general(
                        window(tap),
                        jnp.concatenate([rows[1], pair_rows[...]], axis=0),
                        (((0,), (0,)), ((), ())),
                        preferred_element_type=F32,
                    )

            @pl.when(core == 1)
            def _():
                @pl.loop(start, stop)
                def _(tap):
                    term[pl.ds(pl.multiple_of(tap * C, C), C), :] = jnp.dot(
                        turned[...], window(26 - tap), preferred_element_type=F32
                    )

        reduce.begin(piece, upper)
        if upper:
            reduce.advance()
        elif piece:
            reduce.relay_lower(piece - 1)
    for field in range(2):
        for copy in faces[2 + field]:
            copy.wait_recv()
        build_windows(landed[1, field], rows[field], placing, win.at[1, field])
    reduce.advance()
    out_ref[...] = jnp.where(live, conv(win.at[1, 0], w2), 0.0)
    puts = [
        pltpu.make_async_copy(source, target, put_sems.at[index])
        for index, (source, target) in enumerate(
            (
                (out_ref, out_hbm),
                (grad_ref, grad_hbm),
                (first_ref, first_hbm),
                (second_ref, second_hbm),
            )
        )
    ]
    puts[0].start()
    reduce.advance()
    grad_ref[...] = jnp.where(live, conv_back(win.at[1, 1], w1), 0.0)
    puts[1].start()
    while reduce.advance():
        pass
    reduce.finish(first_ref, second_ref)
    for put in puts[2:]:
        put.start()
    for copy in code_copies + sum(faces, []) + pair:
        copy.wait_send()
    reduce.drain()
    for put in puts:
        put.wait()


def store_kernel(*refs):
    sources, targets, held, sems = refs[:4], refs[4:8], refs[8:12], refs[12]
    takes = [
        pltpu.make_async_copy(sources[index], held[index], sems.at[index]) for index in range(4)
    ]
    puts = [
        pltpu.make_async_copy(held[index], targets[index], sems.at[4 + index])
        for index in range(4)
    ]
    for take in takes:
        take.start()
    for take, put in zip(takes, puts):
        take.wait()
        put.start()
    for put in puts:
        put.wait()


def vmem():
    return pl.BlockSpec(memory_space=pltpu.VMEM)


def smem():
    return pl.BlockSpec(memory_space=pltpu.SMEM)


def hbm():
    return pl.BlockSpec(memory_space=pltpu.HBM)


def per_device(features, block_coords, block_counts, first_weight, second_weight, cotangent):
    feat = features.reshape(ROWS, C)
    cot = cotangent.reshape(ROWS, C)
    coords = block_coords.reshape(1, SLOTS)
    counts = block_counts.reshape(1, 1)
    pick_np, table_np = face_tables()
    pick = jnp.asarray(pick_np, BF16)
    table = jnp.asarray(table_np)
    struct = jax.ShapeDtypeStruct
    scale = 1.0 / math.sqrt(64 * SLOTS * lax.axis_size("gx") * lax.axis_size("gy"))
    nz = lax.axis_size("gx") // 4
    window = (9, SLOTS, 6, 16, C)
    dma = pltpu.SemaphoreType.DMA
    out, grad, first_grad, second_grad = pl.pallas_call(
        functools.partial(step_kernel, nz, scale),
        out_shape=(
            struct((ROWS, C), F32),
            struct((ROWS, C), F32),
            struct((32, BLOCK), F32),
            struct((32, BLOCK), F32),
        ),
        in_specs=[hbm()] * 4 + [smem()] * 2 + [hbm()] * 2,
        out_specs=(hbm(),) * 4,
        scratch_shapes=[
            pltpu.VMEM((ROWS, C), F32),
            pltpu.VMEM((ROWS, C), F32),
            pltpu.VMEM((32, BLOCK), F32),
            pltpu.VMEM((32, BLOCK), F32),
            dma((4,)),
            pltpu.VMEM((ROWS, C), BF16),
            pltpu.VMEM((ROWS, C), BF16),
            pltpu.VMEM((2, FACE, ROWS), BF16),
            pltpu.VMEM((FACE, ROWS), BF16),
            pltpu.VMEM((8, DATA), jnp.int32),
            pltpu.VMEM((27 * C, C), BF16),
            pltpu.VMEM((27 * C, C), BF16),
            dma((6,)),
            pltpu.VMEM((2, 2, FACE, C), BF16),
            pltpu.VMEM((2, 2, FACE, C), BF16),
            dma((2, 2, 8)),
            dma((2, 2, 8)),
            pltpu.VMEM((8, DATA), jnp.int32),
            pltpu.VMEM((8, 8, DATA), jnp.int32),
            dma((8,)),
            dma((8,)),
            pltpu.VMEM((9, 96 * SLOTS, DATA), BF16),
            pltpu.VMEM((2, 2) + window, BF16),
            pltpu.VMEM((2, ROWS, C), BF16),
            pltpu.VMEM(window, BF16),
            pltpu.VMEM((ROWS, C), BF16),
            dma((4,)),
            pltpu.VMEM((C, 2 * ROWS), BF16),
            pltpu.VMEM((27 * C, C), F32),
        ]
        + reduce_scratch(nz),
        compiler_params=pltpu.CompilerParams(
            collective_id=0, has_side_effects=True, vmem_limit_bytes=LIMIT
        ),
        name="step",
    )(feat, cot, pick, table, coords, counts, first_weight, second_weight)
    results = (out, grad, first_grad, second_grad)
    out, grad, first_grad, second_grad = pl.pallas_call(
        store_kernel,
        out_shape=[struct(result.shape, F32) for result in results],
        in_specs=[hbm()] * 4,
        out_specs=[hbm()] * 4,
        scratch_shapes=[pltpu.VMEM(result.shape, F32) for result in results] + [dma((8,))],
        name="store",
    )(*results)
    return out.reshape(features.shape), grad.reshape(features.shape), first_grad.T, second_grad.T


def solution(mesh):
    placed = (
        P("gx", "gy", None, None, None),
        P("gx", "gy", None),
        P("gx", "gy"),
        P(),
        P(),
        P("gx", "gy", None, None, None),
    )
    return jax.shard_map(
        per_device,
        mesh=mesh,
        in_specs=placed,
        out_specs=(
            P("gx", "gy", None, None, None),
            P("gx", "gy", None, None, None),
            P("gx", "gy"),
            P("gx", "gy"),
        ),
        check_vma=False,
    )
```
